128 devices in a mesh: lat: 8 (over z, core), lon: 16 (over y, x).
Axes of the slice: x: 4, y: 4, z: 4, core: 2. Of those that a mesh axis runs over, the one named last changes fastest.
Arguments:
- tokens: bfloat16 [128, 1024, 512], P('lat', 'lon'), may hold values from -6 to 6
- norm_gain: float32 [512], replicated, may hold values from 0.25 to 1.75
- w_query: bfloat16 [512, 512], replicated, may hold values from -1 to 1
- w_key: bfloat16 [512, 512], replicated, may hold values from -1 to 1
- w_value: bfloat16 [512, 512], replicated, may hold values from -0.25 to 0.25
- w_out: bfloat16 [512, 512], replicated, may hold values from -0.25 to 0.25
- pool_weight: bfloat16 [4, 64], replicated, may hold values from -0.75 to 0.75
- head_scale: float32 [8], replicated, may hold values from 0.5 to 32
- far_ids: int32 [16, 128, 48], P('lat', 'lon'), may hold values from 0 to 2047, as said below
- far_mask: int32 [16, 128, 48], P('lat', 'lon'), may hold values from 0 to 1, as said below
- mlp_gain: float32 [512], replicated, may hold values from 0.25 to 1.75
- w_up: bfloat16 [512, 2048], replicated, may hold values from -0.25 to 0.25
- w_down: bfloat16 [2048, 512], replicated, may hold values from -0.125 to 0.125
Outputs:
- result: bfloat16 [128, 1024, 512], P('lat', 'lon')
The draws below stay inside these ranges and needn't reach their ends.
Inputs may be any that keep to these rules, and one draw needn't show every extreme that they name: `far_mask`: used slots come first in each block's list; every block uses at least 12 slots. `far_ids`: the tile of 16 x 64 tokens that one device holds is a grid of blocks; among all list slots of one such tile, used or not, the blocks of any one tile are named at most 6 times, and exactly 6 times for some tiles.
All inputs are finite; a program needn't handle non-finite values.
Results may differ from the reference program's by a relative error of at most 0.006.
The reference program's roundings to bfloat16 on the way count: a program that leaves them out, or rounds other values in their place, can miss the bound.
Values may be sent and summed in bfloat16 or wider, within the bound.
A program may use at most 128 MiB of HBM per device.

```python
import math
import jax
import jax.numpy as jnp
from jax import lax

D = 512
HEADS = 8
FF = 2048
BLK = 8
SUMROWS = 4
FAR = 48
ROWS_DEV = 16
COLS_DEV = 64
NROWS = 128
NCOLS = 1024
BLAT = 16
BLON = 128
NBLK = 2048
N_LAT = 8
N_LON = 16


def query_key_pair(key):
    first = jax.random.normal(jax.random.fold_in(key, 11), (D, D), jnp.float32) / jnp.sqrt(jnp.float32(D))
    second = jax.random.normal(jax.random.fold_in(key, 12), (D, D), jnp.float32) / jnp.sqrt(jnp.float32(D))
    return (first, second)


def draw_w_query(key, part):
    first, second = query_key_pair(key)
    return first.astype(jnp.bfloat16)


def draw_w_key(key, part):
    first, second = query_key_pair(key)
    mixed = second
    return mixed.astype(jnp.bfloat16)


def draw_head_scale(key, part):
    uniform_part = jax.random.uniform(jax.random.fold_in(key, 41), (HEADS,), jnp.float32)
    lower = jnp.log(jnp.float32(0.5))
    upper = jnp.log(jnp.float32(2.0))
    return jnp.exp(lower + (upper - lower) * uniform_part).astype(jnp.float32)


def draw_tokens(key, part):
    base = jax.random.normal(jax.random.fold_in(key, 21), (NROWS, NCOLS, D), jnp.float32)
    return jnp.clip(base, -6.0, 6.0).astype(jnp.bfloat16)


def draw_far_mask(key, part):
    lat_rows = jnp.arange(BLAT, dtype=jnp.int32)
    polar = jnp.abs(2 * lat_rows + 1 - BLAT)
    lowest = FAR // 4
    base_count = lowest + (FAR - lowest) * polar // BLAT
    extra = jax.random.randint(jax.random.fold_in(key, 31), (BLAT, BLON), 0, lowest + 1)
    used = jnp.minimum(base_count[:, None] + extra, FAR)
    slots = jnp.arange(FAR, dtype=jnp.int32)
    return (slots[None, None, :] < used[:, :, None]).astype(jnp.int32)


def draw_far_ids(key, part):
    tile_rows = ROWS_DEV // BLK
    tile_cols = COLS_DEV // BLK
    tile_blocks = tile_rows * tile_cols
    slot_count = tile_blocks * FAR
    device_count = N_LAT * N_LON
    keys = jax.random.split(jax.random.fold_in(key, 51), device_count)
    orders = jax.vmap(lambda one: jax.random.permutation(one, slot_count))(keys).astype(jnp.int32)
    owner = orders % device_count
    inside = jax.random.randint(jax.random.fold_in(key, 52), (device_count, slot_count), 0, tile_blocks)
    grow = owner // N_LON * tile_rows + inside // tile_cols
    gcol = owner % N_LON * tile_cols + inside % tile_cols
    numbers = (grow * BLON + gcol).astype(jnp.int32)
    shaped = numbers.reshape(N_LAT, N_LON, tile_rows, tile_cols, FAR).transpose(0, 2, 1, 3, 4)
    return shaped.reshape(BLAT, BLON, FAR)


def gaussian(key, dims, deviation, most, kind=jnp.bfloat16):
    drawn = jax.random.normal(key, dims, jnp.float32) * deviation
    return jnp.minimum(jnp.maximum(drawn, -most), most).astype(kind)


def setup_inputs(seed: int = 0) -> dict:
    key_list = jax.random.split(jax.random.key(seed), 14)
    return {
        "tokens": draw_tokens(jax.random.fold_in(key_list[13], 71), 0),
        "norm_gain": jnp.clip(1.0 + 0.15 * jax.random.normal(key_list[1], (D,), jnp.float32), 0.25, 1.75),
        "w_query": draw_w_query(jax.random.fold_in(key_list[13], 71), 0),
        "w_key": draw_w_key(jax.random.fold_in(key_list[13], 71), 0),
        "w_value": gaussian(key_list[4], (D, D), D ** -0.5, 0.25),
        "w_out": gaussian(key_list[5], (D, D), D ** -0.5, 0.25),
        "pool_weight": gaussian(key_list[6], (SUMROWS, BLK * BLK), (BLK * BLK) ** -0.5, 0.75),
        "head_scale": draw_head_scale(jax.random.fold_in(key_list[13], 71), 0),
        "far_ids": draw_far_ids(jax.random.fold_in(key_list[13], 71), 0),
        "far_mask": draw_far_mask(jax.random.fold_in(key_list[13], 71), 0),
        "mlp_gain": jnp.clip(1.0 + 0.15 * jax.random.normal(key_list[10], (D,), jnp.float32), 0.25, 1.75),
        "w_up": gaussian(key_list[11], (D, FF), D ** -0.5, 0.25),
        "w_down": gaussian(key_list[12], (FF, D), FF ** -0.5, 0.125),
    }


eps = 1e-06

def rms_scale(values, scale_gain):
    wide = values.astype(jnp.float32)
    mean_square = lax.optimization_barrier(jnp.mean(wide * wide, axis=-1, keepdims=True))
    return (wide * lax.rsqrt(mean_square + eps) * scale_gain).astype(jnp.bfloat16)

def project(values, weight):
    flat = values.reshape(-1, values.shape[-1])
    output = jnp.dot(flat, weight, preferred_element_type=jnp.float32).astype(jnp.bfloat16)
    return output.reshape(values.shape[:-1] + (weight.shape[1],))

def to_blocks(grid):
    row_count, col_count, feature = grid.shape
    shaped = grid.reshape(row_count // BLK, BLK, col_count // BLK, BLK, feature)
    return shaped.transpose(0, 2, 1, 3, 4).reshape(row_count // BLK, col_count // BLK, BLK * BLK, feature)

def neighbours(strip):
    col_count = strip.shape[1] - 2 * BLK
    feature = strip.shape[2]
    pieces = [strip[:, offset * BLK:offset * BLK + col_count].reshape(3 * BLK, col_count // BLK, BLK, feature) for offset in range(3)]
    stacked = jnp.stack(pieces, axis=2)
    return stacked.transpose(1, 0, 2, 3, 4).reshape(col_count // BLK, 9 * BLK * BLK, feature)

def attend(query, key_rows, value_rows, valid, head_scale):
    block_count, query_count, feature = query.shape
    head_count = head_scale.shape[0]
    head_size = feature // head_count
    query_heads = query.astype(jnp.float32).reshape(block_count, query_count, head_count, head_size)
    key_heads = key_rows.astype(jnp.float32).reshape(block_count, -1, head_count, head_size)
    value_heads = value_rows.astype(jnp.float32).reshape(block_count, -1, head_count, head_size)
    score = jnp.einsum('bqhd,bkhd->bhqk', query_heads, key_heads)
    score = score * (head_scale * (1.0 / math.sqrt(head_size)))[None, :, None, None]
    keep = valid[:, None, None, :]
    highest = lax.optimization_barrier(jnp.max(jnp.where(keep, score, -1e+30), axis=-1, keepdims=True))
    expo = jnp.exp(jnp.where(keep, score - highest, -1e+30))
    weights = (expo / lax.optimization_barrier(jnp.sum(expo, axis=-1, keepdims=True))).astype(jnp.bfloat16)
    mixed = jnp.einsum('bhqk,bkhd->bqhd', weights.astype(jnp.float32), value_heads)
    return mixed.astype(jnp.bfloat16).reshape(block_count, query_count, feature)

def reference(tokens, norm_gain, w_query, w_key, w_value, w_out, pool_weight, head_scale, far_ids, far_mask, mlp_gain, w_up, w_down):
    normed = rms_scale(tokens, norm_gain)
    query = project(normed, w_query)
    w_pair = jnp.concatenate([w_key, w_value], axis=1)
    paired = project(normed, w_pair)
    blocks = to_blocks(normed)
    pooled = jnp.einsum('rt,abtd->abrd', pool_weight.astype(jnp.float32), blocks.astype(jnp.float32)).astype(jnp.bfloat16)
    summary = project(pooled, w_pair).reshape(NBLK, SUMROWS, 2 * D)
    wrapped = jnp.concatenate([paired[:, NCOLS - BLK:], paired, paired[:, :BLK]], axis=1)
    padded = jnp.pad(wrapped, ((BLK, BLK), (0, 0), (0, 0)))
    place = jnp.arange(NROWS + 2 * BLK, dtype=jnp.int32)
    row_valid = (place >= BLK) & (place < NROWS + BLK)
    query_blocks = to_blocks(query)

    def one_row(row_index):
        strip = lax.dynamic_slice_in_dim(padded, row_index * BLK, 3 * BLK, 0)
        near = neighbours(strip)
        strip_valid = lax.dynamic_slice_in_dim(row_valid, row_index * BLK, 3 * BLK, 0)
        near_valid = jnp.broadcast_to(strip_valid[:, None, None], (3 * BLK, 3, BLK)).reshape(-1)
        listed = far_ids[row_index].reshape(-1).astype(jnp.int32)
        far_rows = jnp.take(summary, listed, axis=0).reshape(BLON, FAR * SUMROWS, 2 * D)
        far_valid = jnp.repeat(far_mask[row_index] > 0, SUMROWS, axis=1)
        valid = jnp.concatenate([jnp.broadcast_to(near_valid[None, :], (BLON, near_valid.shape[0])), far_valid], axis=1)
        key_rows = jnp.concatenate([near[..., :D], far_rows[..., :D]], axis=1)
        value_rows = jnp.concatenate([near[..., D:], far_rows[..., D:]], axis=1)
        return attend(query_blocks[row_index], key_rows, value_rows, valid, head_scale)
    attended = lax.map(one_row, jnp.arange(BLAT, dtype=jnp.int32))
    attn = attended.reshape(BLAT, BLON, BLK, BLK, D).transpose(0, 2, 1, 3, 4).reshape(NROWS * NCOLS, D)
    mixed = (tokens.reshape(-1, D).astype(jnp.float32) + jnp.dot(attn, w_out, preferred_element_type=jnp.float32)).astype(jnp.bfloat16)
    normed_two = rms_scale(mixed, mlp_gain)
    hidden = jax.nn.gelu(jnp.dot(normed_two, w_up, preferred_element_type=jnp.float32), approximate=True).astype(jnp.bfloat16)
    result = (mixed.astype(jnp.float32) + jnp.dot(hidden, w_down, preferred_element_type=jnp.float32)).astype(jnp.bfloat16)
    return result.reshape(NROWS, NCOLS, D)
```

```python
import functools
import math

import jax
import jax.numpy as jnp
from jax import lax
from jax.experimental import pallas as pl
from jax.experimental.pallas import tpu as pltpu
from jax.sharding import PartitionSpec as P

BLK = 8
TOK = BLK * BLK
SUMROWS = 4
FAR = 48
EPS = 1e-06
NEG = -1e30
LOG2E = 1.4426950408889634
F32 = jnp.float32
BF16 = jnp.bfloat16


def rms(wide, gain):
    mean_square = jnp.mean(wide * wide, axis=-1, keepdims=True)
    return (wide * lax.rsqrt(mean_square + EPS) * gain).astype(BF16)


def blocks_of_rows(rows):
    count = rows[0].shape[0] // BLK
    return [
        jnp.concatenate([row[j * BLK : (j + 1) * BLK] for row in rows], axis=0)
        for j in range(count)
    ]


def pool_kernel(tok_ref, gain_ref, pool_ref, out_ref):
    gain = gain_ref[...]
    blocks = blocks_of_rows([tok_ref[r].astype(F32) for r in range(BLK)])
    for j, block in enumerate(blocks):
        normed = rms(block, gain)
        pooled = jnp.dot(pool_ref[...], normed, preferred_element_type=F32)
        out_ref[j] = pooled.astype(BF16)


def pool_call(tokens, gain, pool_weight):
    rows, cols, feature = tokens.shape
    blk_rows, blk_cols = rows // BLK, cols // BLK
    return pl.pallas_call(
        pool_kernel,
        grid=(blk_rows,),
        in_specs=[
            pl.BlockSpec((BLK, cols, feature), lambda i: (i, 0, 0)),
            pl.BlockSpec((1, feature), lambda i: (0, 0)),
            pl.BlockSpec((SUMROWS, TOK), lambda i: (0, 0)),
        ],
        out_specs=pl.BlockSpec((blk_cols, SUMROWS, feature), lambda i: (i, 0, 0)),
        out_shape=jax.ShapeDtypeStruct((blk_rows * blk_cols, SUMROWS, feature), BF16),
        name="pool",
    )(tokens, gain.reshape(1, feature), pool_weight)


def qkv_kernel(
    tok_ref, up_ref, down_ref, left_ref, right_ref, ul_ref, ur_ref, dl_ref, dr_ref,
    gain_ref, wq_ref, wk_ref, wv_ref, q_ref, k_ref, v_ref, nb_ref,
):
    gain = gain_ref[...]
    for bi in range(4):
        if bi == 0:
            mid, lt, rt = up_ref, ul_ref, ur_ref
            base = 0
        elif bi == 3:
            mid, lt, rt = down_ref, dl_ref, dr_ref
            base = 0
        else:
            mid, lt, rt = tok_ref, left_ref, right_ref
            base = (bi - 1) * BLK
        left = blocks_of_rows([lt[base + r].astype(F32) for r in range(BLK)])
        middle = blocks_of_rows([mid[base + r].astype(F32) for r in range(BLK)])
        right = blocks_of_rows([rt[base + r].astype(F32) for r in range(BLK)])
        for bj, block in enumerate(left + middle + right):
            nb_ref[bj * TOK : (bj + 1) * TOK, :] = rms(block, gain)
        k_ref[bi] = jnp.dot(nb_ref[...], wk_ref[...], preferred_element_type=F32).astype(BF16)
        v_ref[bi] = jnp.dot(nb_ref[...], wv_ref[...], preferred_element_type=F32).astype(BF16)
        if bi in (1, 2):
            local = nb_ref[TOK : TOK + 8 * TOK, :]
            q_ref[bi - 1] = jnp.dot(local, wq_ref[...], preferred_element_type=F32).astype(BF16)


def qkv_call(tokens, halos, gain, w_query, w_key, w_value):
    rows, cols, feature = tokens.shape
    blk_cols = cols // BLK
    wide = (blk_cols + 2) * TOK
    return pl.pallas_call(
        qkv_kernel,
        out_shape=(
            jax.ShapeDtypeStruct((2, blk_cols * TOK, feature), BF16),
            jax.ShapeDtypeStruct((4, wide, feature), BF16),
            jax.ShapeDtypeStruct((4, wide, feature), BF16),
        ),
        scratch_shapes=[pltpu.VMEM((wide, feature), BF16)],
        compiler_params=pltpu.CompilerParams(vmem_limit_bytes=40 << 20),
        cost_estimate=pl.CostEstimate(
            flops=2 * (2 * 4 * wide + rows * cols) * feature * feature,
            bytes_accessed=8 << 20,
            transcendentals=0,
        ),
        name="qkv",
    )(tokens, *halos, gain.reshape(1, feature), w_query, w_key, w_value)


def gelu(x):
    return jax.nn.gelu(x, approximate=True)


def main_kernel(
    idx_ref, scale_ref, bias_ref, q_ref, k_ref, v_ref, pooled_ref, wk_ref, wv_ref, mgain_ref,
    tok_hbm, wout_hbm, wup_hbm, wdown_hbm,
    out_ref,
    far_ref, kf_ref, vf_ref, attn_ref, tok_ref, wout_ref, wup_ref, wdown_ref, sems,
):
    copies = [
        pltpu.make_async_copy(src, dst, sems.at[n])
        for n, (src, dst) in enumerate(
            ((tok_hbm, tok_ref), (wout_hbm, wout_ref), (wup_hbm, wup_ref), (wdown_hbm, wdown_ref))
        )
    ]
    for copy in copies:
        copy.start()
    lane_head = lax.broadcasted_iota(jnp.int32, (TOK, 256), 1) // TOK

    for i in range(2):
        order = (1, 2, 0) if i == 0 else (0, 1, 2)

        def one_block(j, carry):
            b = i * 8 + j
            for s in range(FAR):
                far_ref[s * SUMROWS : (s + 1) * SUMROWS, :] = pooled_ref[idx_ref[b, s]]
            far = far_ref[...]
            kf_ref[...] = jnp.dot(far, wk_ref[...], preferred_element_type=F32).astype(BF16)
            vf_ref[...] = jnp.dot(far, wv_ref[...], preferred_element_type=F32).astype(BF16)
            start = pl.multiple_of(j * TOK, TOK)
            bias = bias_ref[b]
            for g in range(2):
                feats = slice(g * 256, (g + 1) * 256)
                query = q_ref[i, pl.ds(start, TOK), feats]
                stacked = jnp.concatenate(
                    [jnp.where(lane_head == h, query, jnp.zeros_like(query)) for h in range(4)], axis=0
                )
                keys = jnp.concatenate(
                    [k_ref[i + d, pl.ds(start, 3 * TOK), feats] for d in order] + [kf_ref[:, feats]], axis=0
                )
                values = jnp.concatenate(
                    [v_ref[i + d, pl.ds(start, 3 * TOK), feats] for d in order] + [vf_ref[:, feats]], axis=0
                )
                score = lax.dot_general(
                    stacked, keys, (((1,), (1,)), ((), ())), preferred_element_type=F32
                )
                weights = []
                for h in range(4):
                    part = score[h * TOK : (h + 1) * TOK]
                    part = jnp.concatenate([part[:, :384], part[:, 384:] + bias], axis=1)
                    highest = jnp.max(part, axis=-1, keepdims=True)
                    expo = jnp.exp2((part - highest) * scale_ref[0, g * 4 + h])
                    total = jnp.sum(expo, axis=-1, keepdims=True)
                    weights.append((expo * (1.0 / total)).astype(BF16))
                weight = jnp.concatenate(weights, axis=0)
                full = jnp.dot(weight, values, preferred_element_type=F32)
                picked = jnp.zeros((TOK, 256), F32)
                for h in range(4):
                    picked = jnp.where(lane_head == h, full[h * TOK : (h + 1) * TOK], picked)
                attn_ref[i, pl.ds(start, TOK), feats] = picked.astype(BF16)
            return carry

        lax.fori_loop(0, 8, one_block, 0)

    for copy in copies:
        copy.wait()
    mgain = mgain_ref[...]
    for i in range(2):
        token_blocks = blocks_of_rows([tok_ref[i * BLK + r].astype(F32) for r in range(BLK)])
        for half in range(2):
            rows = slice(half * 256, (half + 1) * 256)
            token = jnp.concatenate(token_blocks[half * 4 : half * 4 + 4], axis=0)
            mixed = (
                token + jnp.dot(attn_ref[i, rows, :], wout_ref[...], preferred_element_type=F32)
            ).astype(BF16)
            wide = mixed.astype(F32)
            normed = rms(wide, mgain)
            acc = wide
            for f in range(4):
                part = slice(f * 512, (f + 1) * 512)
                hidden = gelu(
                    jnp.dot(normed, wup_ref[:, part], preferred_element_type=F32)
                ).astype(BF16)
                acc = acc + jnp.dot(hidden, wdown_ref[part, :], preferred_element_type=F32)
            for r in range(BLK):
                row = jnp.concatenate(
                    [acc[j * TOK + r * BLK : j * TOK + (r + 1) * BLK] for j in range(4)], axis=0
                )
                out_ref[i * BLK + r, half * 32 : (half + 1) * 32, :] = row.astype(BF16)


def main_call(idx, scale, bias, q, k, v, pooled, w_key, w_value, mlp_gain, tokens, w_out, w_up, w_down):
    rows, cols, feature = tokens.shape
    vmem = pl.BlockSpec(memory_space=pltpu.VMEM)
    smem = pl.BlockSpec(memory_space=pltpu.SMEM)
    hbm = pl.BlockSpec(memory_space=pl.ANY)
    return pl.pallas_call(
        main_kernel,
        out_shape=jax.ShapeDtypeStruct(tokens.shape, BF16),
        in_specs=[smem, smem] + [vmem] * 8 + [hbm] * 4,
        out_specs=vmem,
        scratch_shapes=[
            pltpu.VMEM((FAR * SUMROWS, feature), BF16),
            pltpu.VMEM((FAR * SUMROWS, feature), BF16),
            pltpu.VMEM((FAR * SUMROWS, feature), BF16),
            pltpu.VMEM((2, 8 * TOK, feature), BF16),
            pltpu.VMEM(tokens.shape, BF16),
            pltpu.VMEM(w_out.shape, BF16),
            pltpu.VMEM(w_up.shape, BF16),
            pltpu.VMEM(w_down.shape, BF16),
            pltpu.SemaphoreType.DMA((4,)),
        ],
        compiler_params=pltpu.CompilerParams(vmem_limit_bytes=56 << 20),
        cost_estimate=pl.CostEstimate(
            flops=20_000_000_000, bytes_accessed=24 << 20, transcendentals=6_000_000
        ),
        name="main",
    )(idx, scale, bias, q, k, v, pooled, w_key, w_value, mlp_gain.reshape(1, feature), tokens, w_out, w_up, w_down)


def shifted(value, lat_step, lon_step):
    lat_count, lon_count = lax.axis_size("lat"), lax.axis_size("lon")
    pairs = []
    for a in range(lat_count):
        for o in range(lon_count):
            ta, to = a + lat_step, (o + lon_step) % lon_count
            if 0 <= ta < lat_count:
                pairs.append((a * lon_count + o, ta * lon_count + to))
    return lax.ppermute(value, ("lat", "lon"), pairs)


def local(
    tokens, norm_gain, w_query, w_key, w_value, w_out, pool_weight, head_scale,
    far_ids, far_mask, mlp_gain, w_up, w_down,
):
    rows, cols, feature = tokens.shape
    blk_rows, blk_cols = rows // BLK, cols // BLK
    heads = head_scale.shape[0]
    lat_count, lon_count = lax.axis_size("lat"), lax.axis_size("lon")
    lat_index = lax.axis_index("lat")
    pooled = pool_call(tokens, norm_gain, pool_weight)
    every = lax.all_gather(pooled, ("lat", "lon"), axis=0, tiled=True)
    up = shifted(tokens[rows - BLK :], 1, 0)
    down = shifted(tokens[:BLK], -1, 0)
    left = shifted(tokens[:, cols - BLK :], 0, 1)
    right = shifted(tokens[:, :BLK], 0, -1)
    ul = shifted(tokens[rows - BLK :, cols - BLK :], 1, 1)
    ur = shifted(tokens[rows - BLK :, :BLK], 1, -1)
    dl = shifted(tokens[:BLK, cols - BLK :], -1, 1)
    dr = shifted(tokens[:BLK, :BLK], -1, -1)
    q, k, v = qkv_call(
        tokens, (up, down, left, right, ul, ur, dl, dr), norm_gain, w_query, w_key, w_value
    )
    global_cols = blk_cols * lon_count
    global_row = far_ids // global_cols
    global_col = far_ids % global_cols
    owner = global_row // blk_rows * lon_count + global_col // blk_cols
    inner_block = global_row % blk_rows * blk_cols + global_col % blk_cols
    idx = (owner * (blk_rows * blk_cols) + inner_block).reshape(blk_rows * blk_cols, FAR)
    far_valid = jnp.repeat(far_mask.reshape(blk_rows * blk_cols, FAR) > 0, SUMROWS, axis=1)
    block_row = jnp.arange(blk_rows * blk_cols) // blk_cols
    edge_ok = jnp.where(block_row == 0, lat_index > 0, lat_index < lat_count - 1)
    valid = jnp.concatenate(
        [jnp.broadcast_to(edge_ok[:, None], (blk_rows * blk_cols, 3 * TOK)), far_valid], axis=1
    )
    bias = jnp.where(valid, 0.0, NEG).astype(F32)[:, None, :]
    scale = (head_scale * (LOG2E / math.sqrt(feature // heads))).reshape(1, heads)
    return main_call(
        idx, scale, bias, q, k, v, every, w_key, w_value, mlp_gain, tokens, w_out, w_up, w_down
    )


def solution(mesh):
    return jax.shard_map(
        local,
        mesh=mesh,
        in_specs=(
            P("lat", "lon", None),
            P(), P(), P(), P(), P(), P(), P(),
            P("lat", "lon", None),
            P("lat", "lon", None),
            P(), P(), P(),
        ),
        out_specs=P("lat", "lon", None),
        check_vma=False,
    )
```

```python
import math

import jax
import jax.numpy as jnp
from jax import lax
from jax.experimental import pallas as pl
from jax.experimental.pallas import tpu as pltpu
from jax.sharding import PartitionSpec as P

BLK = 8
TOK = BLK * BLK
SUMROWS = 4
FAR = 48
EPS = 1e-06
NEG = -1e30
LOG2E = 1.4426950408889634
F32 = jnp.float32
BF16 = jnp.bfloat16
MESH = pl.DeviceIdType.MESH

RING = 4
PARTS = (6, 5, 5)
FIRST = (0, 6, 11)
AXES = (("x", "y", "z"), ("y", "z", "x"), ("z", "x", "y"))
COLS = 8
WIDE = (COLS + 2) * TOK
ROW = COLS * TOK


def rms(wide, gain):
    mean_square = jnp.mean(wide * wide, axis=-1, keepdims=True)
    return (wide * lax.rsqrt(mean_square + EPS) * gain).astype(BF16)


def dot(a, b):
    return jnp.dot(a, b, preferred_element_type=F32)


def summary_row(core, spot, inner):
    row = None
    for part in range(3):
        first, second, third = (spot[axis] for axis in AXES[part])
        place = ((core * RING + third) * RING + second) * RING + first
        here = 128 * FIRST[part] + place * PARTS[part] + inner - FIRST[part]
        row = here if row is None else jnp.where(inner >= FIRST[part], here, row)
    return row


class Gather:
    def __init__(self, ref, send, recv, sib_send, sib_recv, core, spot, lat, lon):
        self.ref = ref
        self.send, self.recv = send, recv
        self.sib_send, self.sib_recv = sib_send, sib_recv
        self.core, self.spot = core, spot
        self.lat, self.lon = lat, lon
        self.started = []

    def device(self, axis, step):
        spot = dict(self.spot)
        spot[axis] = (spot[axis] + step + RING) % RING
        return (2 * spot["z"] + self.core, RING * spot["y"] + spot["x"])

    def rows(self, part, phase, step, half=None, core=None):
        axis = AXES[part][phase]
        spot = dict(self.spot)
        spot[axis] = (spot[axis] + step + RING) % RING
        core = self.core if core is None else core
        place = core
        for level in (2, 1, 0):
            if level >= phase:
                place = place * RING + spot[AXES[part][level]]
        size = PARTS[part] * RING**phase
        start = 128 * FIRST[part] + place * size
        cut = (size + 1) // 2
        if half == 0:
            size = cut
        elif half == 1:
            start, size = start + cut, size - cut
        return pl.ds(start, size)

    def copy(self, rows, send, recv, device):
        return pltpu.make_async_remote_copy(
            src_ref=self.ref.at[rows],
            dst_ref=self.ref.at[rows],
            send_sem=send,
            recv_sem=recv,
            device_id=device,
            device_id_type=MESH,
        )

    def ring(self, part, phase, kind, start):
        axis = AXES[part][phase]
        step = 1 if kind in (0, 2) else -1
        if start:
            origin, half = (0, None) if kind < 2 else (-step, kind - 2)
        else:
            origin, half = (-step, None) if kind < 2 else (-2 * step, kind - 2)
        return self.copy(
            self.rows(part, phase, origin, half),
            self.send.at[part, phase, kind],
            self.recv.at[part, phase, kind],
            self.device(axis, step),
        )

    def sibling(self, part, slot, core):
        if slot == 0:
            rows = self.rows(part, 2, 0, None, core)
        else:
            kind = slot - 1
            step = 1 if kind in (0, 2) else -1
            origin, half = (-step, None) if kind < 2 else (-2 * step, kind - 2)
            rows = self.rows(part, 2, origin, half, core)
        other = (self.lat + 1 - 2 * self.core, self.lon)
        return self.copy(rows, self.sib_send.at[part, slot], self.sib_recv.at[part, slot], other)

    def start_ring(self, phase, kinds):
        for kind in kinds:
            for part in range(3):
                copy = self.ring(part, phase, kind, True)
                copy.start()
                self.started.append(copy)

    def wait_ring(self, phase, kinds):
        for kind in kinds:
            for part in range(3):
                self.ring(part, phase, kind, False).wait_recv()

    def start_sibling(self, slots):
        for slot in slots:
            for part in range(3):
                copy = self.sibling(part, slot, self.core)
                copy.start()
                self.started.append(copy)

    def wait_sibling(self):
        for slot in range(5):
            for part in range(3):
                self.sibling(part, slot, 1 - self.core).wait_recv()

    def finish(self):
        for copy in self.started:
            copy.wait_send()


def layer_kernel(
    idx_ref, scale_ref, bias_ref, gain_ref, mgain_ref, pool_ref,
    tok_hbm, wq_hbm, wk_hbm, wv_hbm, wout_hbm, wup_hbm, wdown_hbm,
    out_ref,
    tok_ref, up_ref, down_ref, left_ref, right_ref, corner_ref,
    wq_ref, wk_ref, wv_ref, wout_ref, wup_ref, wdown_ref,
    every_ref, nb_ref, q_ref, k_ref, v_ref, far_ref, near_ref, high_ref, total_ref, attn_ref,
    load_sem, halo_send, halo_recv, ring_send, ring_recv, sib_send, sib_recv,
):
    lat, lon = lax.axis_index("lat"), lax.axis_index("lon")
    lats, lons = 8, 16
    core = lat % 2
    spot = {"x": lon % RING, "y": lon // RING, "z": lat // 2}
    gather = Gather(every_ref, ring_send, ring_recv, sib_send, sib_recv, core, spot, lat, lon)

    loads = [
        pltpu.make_async_copy(src, dst, load_sem.at[n])
        for n, (src, dst) in enumerate(
            (
                (tok_hbm, tok_ref), (wq_hbm, wq_ref), (wk_hbm, wk_ref), (wv_hbm, wv_ref),
                (wout_hbm, wout_ref), (wup_hbm, wup_ref), (wdown_hbm, wdown_ref),
            )
        )
    ]
    for load in loads:
        load.start()

    def tile(lat_step, lon_step):
        return ((lat + lat_step + lats) % lats, (lon + lon_step + lons) % lons)

    halos = (
        (tok_hbm.at[BLK : 2 * BLK], up_ref, tile(1, 0)),
        (tok_hbm.at[0:BLK], down_ref, tile(-1, 0)),
        (tok_hbm.at[:, COLS - 1], left_ref, tile(0, 1)),
        (tok_hbm.at[:, 0], right_ref, tile(0, -1)),
        (tok_hbm.at[BLK : 2 * BLK, COLS - 1], corner_ref.at[0], tile(1, 1)),
        (tok_hbm.at[BLK : 2 * BLK, 0], corner_ref.at[1], tile(1, -1)),
        (tok_hbm.at[0:BLK, COLS - 1], corner_ref.at[2], tile(-1, 1)),
        (tok_hbm.at[0:BLK, 0], corner_ref.at[3], tile(-1, -1)),
    )
    halo_copies = [
        pltpu.make_async_remote_copy(
            src_ref=src, dst_ref=dst, send_sem=halo_send.at[n], recv_sem=halo_recv.at[n],
            device_id=device, device_id_type=MESH,
        )
        for n, (src, dst, device) in enumerate(halos)
    ]
    partners = [device for _, _, device in halos]
    partners += [gather.device(axis, step) for axis in ("x", "y", "z") for step in (1, -1)]
    partners += [(lat + 1 - 2 * core, lon)]
    barrier = pltpu.get_barrier_semaphore()
    for partner in partners:
        pl.semaphore_signal(barrier, inc=1, device_id=partner, device_id_type=MESH)

    gain = gain_ref[...]
    pool_weight = pool_ref[...]
    loads[0].wait()

    def block_of(ref, first, column):
        return jnp.concatenate([ref[first + r, column].astype(F32) for r in range(BLK)], axis=0)

    for part in range(3):
        base = gather.rows(part, 0, 0).start

        def pool_block(n, carry):
            b = n + FIRST[part]
            i, j = b // COLS, b % COLS
            normed = rms(block_of(tok_ref, i * BLK, j), gain)
            nb_ref[i + 1, pl.ds(pl.multiple_of((j + 1) * TOK, TOK), TOK), :] = normed
            every_ref[base + n] = dot(pool_weight, normed).astype(BF16)
            return carry

        lax.fori_loop(0, PARTS[part], pool_block, 0)
    pl.semaphore_wait(barrier, len(partners))
    for copy in halo_copies:
        copy.start()
    gather.start_ring(0, (0, 1))

    inner = slice(TOK, TOK + ROW)
    loads[1].wait()
    loads[2].wait()
    loads[3].wait()

    def local_qkv(i):
        normed = nb_ref[i + 1, inner, :]
        q_ref[i] = dot(normed, wq_ref[...]).astype(BF16)
        k_ref[i + 1, inner, :] = dot(normed, wk_ref[...]).astype(BF16)
        v_ref[i + 1, inner, :] = dot(normed, wv_ref[...]).astype(BF16)

    local_qkv(0)
    gather.wait_ring(0, (0, 1))
    gather.start_ring(0, (2, 3))
    local_qkv(1)
    gather.wait_ring(0, (2, 3))
    gather.start_ring(1, (0, 1))

    for copy in halo_copies:
        copy.wait_recv()

    def outer_kv(bi, rows):
        normed = nb_ref[bi, rows, :]
        k_ref[bi, rows, :] = dot(normed, wk_ref[...]).astype(BF16)
        v_ref[bi, rows, :] = dot(normed, wv_ref[...]).astype(BF16)

    last = slice(TOK + ROW, WIDE)
    first = slice(0, TOK)

    def outer_row(bi, ref, corner):
        def put(j, carry):
            rows = pl.ds(pl.multiple_of((j + 1) * TOK, TOK), TOK)
            nb_ref[bi, rows, :] = rms(block_of(ref, 0, j), gain)
            return carry

        lax.fori_loop(0, COLS, put, 0, unroll=2)
        for rows, n in ((first, corner), (last, corner + 1)):
            block = jnp.concatenate([corner_ref[n, r].astype(F32) for r in range(BLK)], axis=0)
            nb_ref[bi, rows, :] = rms(block, gain)
        outer_kv(bi, slice(0, WIDE))

    outer_row(0, up_ref, 0)
    gather.wait_ring(1, (0, 1))
    gather.start_ring(1, (2, 3))
    outer_row(3, down_ref, 2)
    for i in range(2):
        for ref, rows in ((left_ref, first), (right_ref, last)):
            block = jnp.concatenate([ref[i * BLK + r].astype(F32) for r in range(BLK)], axis=0)
            nb_ref[i + 1, rows, :] = rms(block, gain)
            outer_kv(i + 1, rows)
    gather.wait_ring(1, (2, 3))
    gather.start_ring(2, (0, 1))
    gather.start_sibling((0,))

    lane_head = lax.broadcasted_iota(jnp.int32, (TOK, 256), 1) // TOK

    def stacked_query(i, rows, feats):
        query = q_ref[i, rows, feats]
        zero = jnp.zeros_like(query)
        return jnp.concatenate([jnp.where(lane_head == h, query, zero) for h in range(4)], axis=0)

    def scores(query, keys):
        return lax.dot_general(query, keys, (((1,), (1,)), ((), ())), preferred_element_type=F32)

    def soft_sum(score, values, scales, bias):
        weights, highs, totals = [], [], []
        for h in range(4):
            part = bias(score[h * TOK : (h + 1) * TOK])
            highest = jnp.max(part, axis=-1, keepdims=True)
            expo = jnp.exp2((part - highest) * scales[h])
            highs.append(highest)
            totals.append(jnp.sum(expo, axis=-1, keepdims=True))
            weights.append(expo.astype(BF16))
        full = dot(jnp.concatenate(weights, axis=0), values)
        picked = full[0:TOK]
        high = jnp.broadcast_to(highs[0], (TOK, 256))
        total = jnp.broadcast_to(totals[0], (TOK, 256))
        for h in range(1, 4):
            mine = lane_head == h
            picked = jnp.where(mine, full[h * TOK : (h + 1) * TOK], picked)
            high = jnp.where(mine, highs[h], high)
            total = jnp.where(mine, totals[h], total)
        return picked, high, total

    def near_block(b, carry):
        i, j = b // COLS, b % COLS
        start = pl.multiple_of(j * TOK, TOK)
        rows = pl.ds(start, TOK)
        around = pl.ds(start, 3 * TOK)
        inside = jnp.where(i == 0, lat > 0, lat < lats - 1)
        edge = jnp.where(inside, jnp.float32(0.0), jnp.float32(NEG))
        for g in range(2):
            feats = slice(g * 256, (g + 1) * 256)
            keys = jnp.concatenate([k_ref[d, around, feats] for d in (1, 2, 3 * i)], axis=0)
            values = jnp.concatenate([v_ref[d, around, feats] for d in (1, 2, 3 * i)], axis=0)
            score = scores(stacked_query(i, rows, feats), keys)
            near_ref[i, rows, feats], high_ref[i, rows, feats], total_ref[i, rows, feats] = soft_sum(
                score, values, [scale_ref[0, g * 4 + h] for h in range(4)],
                lambda part: jnp.concatenate([part[:, :384], part[:, 384:] + edge], axis=1),
            )
        return carry

    lax.fori_loop(0, 8, near_block, 0)
    gather.wait_ring(2, (0, 1))
    gather.start_ring(2, (2, 3))
    gather.start_sibling((1, 2))
    lax.fori_loop(8, 16, near_block, 0)
    gather.wait_ring(2, (2, 3))
    gather.start_sibling((3, 4))
    gather.wait_sibling()

    def far_block(b, carry):
        i, j = b // COLS, b % COLS
        rows = pl.ds(pl.multiple_of(j * TOK, TOK), TOK)
        for s in range(FAR):
            far_ref[s * SUMROWS : (s + 1) * SUMROWS, :] = every_ref[idx_ref[b, s]]
        far = far_ref[...]
        keys = dot(far, wk_ref[...]).astype(BF16)
        values = dot(far, wv_ref[...]).astype(BF16)
        bias = bias_ref[b]
        for g in range(2):
            feats = slice(g * 256, (g + 1) * 256)
            score = scores(stacked_query(i, rows, feats), keys[:, feats])
            scales = [scale_ref[0, g * 4 + h] for h in range(4)]
            far_sum, far_high, far_total = soft_sum(
                score, values[:, feats], scales, lambda part: part + bias
            )
            scale = jnp.full((1, 256), scales[0], F32)
            for h in range(1, 4):
                scale = jnp.where(lane_head[:1] == h, scales[h], scale)
            near_high = high_ref[i, rows, feats]
            high = jnp.maximum(near_high, far_high)
            near_part = jnp.exp2((near_high - high) * scale)
            far_part = jnp.exp2((far_high - high) * scale)
            total = total_ref[i, rows, feats] * near_part + far_total * far_part
            mixed = near_ref[i, rows, feats] * near_part + far_sum * far_part
            attn_ref[i, rows, feats] = (mixed / total).astype(BF16)
        return carry

    lax.fori_loop(0, 16, far_block, 0)

    for load in loads[4:]:
        load.wait()
    mgain = mgain_ref[...]

    def feed_forward(t, carry):
        i, half = t // 2, t % 2
        rows = pl.ds(pl.multiple_of(half * 256, 256), 256)
        token = jnp.concatenate(
            [block_of(tok_ref, i * BLK, half * 4 + j) for j in range(4)], axis=0
        )
        mixed = (token + dot(attn_ref[i, rows, :], wout_ref[...])).astype(BF16)
        wide = mixed.astype(F32)
        normed = rms(wide, mgain)
        acc = wide
        for f in range(4):
            part = slice(f * 512, (f + 1) * 512)
            hidden = jax.nn.gelu(dot(normed, wup_ref[:, part]), approximate=True).astype(BF16)
            acc = acc + dot(hidden, wdown_ref[part, :])
        for r in range(BLK):
            row = jnp.concatenate(
                [acc[j * TOK + r * BLK : j * TOK + (r + 1) * BLK] for j in range(4)], axis=0
            )
            out_ref[i * BLK + r, pl.ds(pl.multiple_of(half * 32, 32), 32), :] = row.astype(BF16)
        return carry

    lax.fori_loop(0, 4, feed_forward, 0)
    for copy in halo_copies:
        copy.wait_send()
    gather.finish()


def layer_call(idx, scale, bias, gain, mgain, pool_weight, tokens, weights):
    rows, cols, feature = tokens.shape
    vmem = pl.BlockSpec(memory_space=pltpu.VMEM)
    smem = pl.BlockSpec(memory_space=pltpu.SMEM)
    hbm = pl.BlockSpec(memory_space=pl.ANY)
    half = (BLK, COLS, BLK, feature)
    dma = pltpu.SemaphoreType.DMA
    return pl.pallas_call(
        layer_kernel,
        out_shape=jax.ShapeDtypeStruct(tokens.shape, BF16),
        in_specs=[smem, smem] + [vmem] * 4 + [hbm] * 7,
        out_specs=vmem,
        scratch_shapes=[
            pltpu.VMEM((2 * BLK, COLS, BLK, feature), BF16),
            pltpu.VMEM(half, BF16),
            pltpu.VMEM(half, BF16),
            pltpu.VMEM((2 * BLK, BLK, feature), BF16),
            pltpu.VMEM((2 * BLK, BLK, feature), BF16),
            pltpu.VMEM((4, BLK, BLK, feature), BF16),
        ]
        + [pltpu.VMEM(weight.shape, BF16) for weight in weights]
        + [
            pltpu.VMEM((2048, SUMROWS, feature), BF16),
            pltpu.VMEM((4, WIDE, feature), BF16),
            pltpu.VMEM((2, ROW, feature), BF16),
            pltpu.VMEM((4, WIDE, feature), BF16),
            pltpu.VMEM((4, WIDE, feature), BF16),
            pltpu.VMEM((FAR * SUMROWS, feature), BF16),
            pltpu.VMEM((2, ROW, feature), F32),
            pltpu.VMEM((2, ROW, feature), F32),
            pltpu.VMEM((2, ROW, feature), F32),
            pltpu.VMEM((2, ROW, feature), BF16),
            dma((7,)), dma((8,)), dma((8,)),
            dma((3, 3, 4)), dma((3, 3, 4)), dma((3, 5)), dma((3, 5)),
        ],
        compiler_params=pltpu.CompilerParams(
            vmem_limit_bytes=60 << 20, collective_id=0, has_side_effects=True
        ),
        name="layer",
    )(
        idx, scale, bias, gain.reshape(1, feature), mgain.reshape(1, feature), pool_weight,
        tokens.reshape(rows, COLS, BLK, feature), *weights,
    )


def local(
    tokens, norm_gain, w_query, w_key, w_value, w_out, pool_weight, head_scale,
    far_ids, far_mask, mlp_gain, w_up, w_down,
):
    rows, cols, feature = tokens.shape
    blk_rows, blk_cols = rows // BLK, cols // BLK
    count = blk_rows * blk_cols
    heads = head_scale.shape[0]
    global_cols = blk_cols * lax.axis_size("lon")
    global_row = far_ids // global_cols
    global_col = far_ids % global_cols
    lat, lon = global_row // blk_rows, global_col // blk_cols
    inner = global_row % blk_rows * blk_cols + global_col % blk_cols
    spot = {"x": lon % RING, "y": lon // RING, "z": lat // 2}
    idx = summary_row(lat % 2, spot, inner).reshape(count, FAR)
    far_valid = jnp.repeat(far_mask.reshape(count, FAR) > 0, SUMROWS, axis=1)
    bias = jnp.where(far_valid, 0.0, NEG).astype(F32)[:, None, :]
    scale = (head_scale * (LOG2E / math.sqrt(feature // heads))).reshape(1, heads)
    return layer_call(
        idx, scale, bias, norm_gain, mlp_gain, pool_weight, tokens,
        (w_query, w_key, w_value, w_out, w_up, w_down),
    )


def solution(mesh):
    return jax.shard_map(
        local,
        mesh=mesh,
        in_specs=(
            P("lat", "lon", None),
            P(), P(), P(), P(), P(), P(), P(),
            P("lat", "lon", None),
            P("lat", "lon", None),
            P(), P(), P(),
        ),
        out_specs=P("lat", "lon", None),
        check_vma=False,
    )
```

```python
import math

import jax
import jax.numpy as jnp
from jax import lax
from jax.experimental import pallas as pl
from jax.experimental.pallas import tpu as pltpu
from jax.sharding import PartitionSpec as P

BLK = 8
TOK = BLK * BLK
SUMROWS = 4
FAR = 48
EPS = 1e-06
NEG = -1e30
SCALE = 1.4426950408889634 / math.sqrt(64)
PUMP_A, PUMP_B, PUMP_C, PUMP_D = 1, 4, 7, 10
F32 = jnp.float32
BF16 = jnp.bfloat16
MESH = pl.DeviceIdType.MESH

RING = 4
PARTS = (4, 5, 7)
FIRST = (0, 4, 9)
AXES = (("x", "y", "z"), ("y", "z", "x"), ("z", "x", "y"))
COLS = 8
WIDE = (COLS + 2) * TOK
ROW = COLS * TOK


def rms(wide, gain):
    mean_square = jnp.mean(wide * wide, axis=-1, keepdims=True)
    return (wide * lax.rsqrt(mean_square + EPS) * gain).astype(BF16)


def dot(a, b):
    return jnp.dot(a, b, preferred_element_type=F32)


def summary_row(core, spot, inner):
    row = None
    for part in range(3):
        first, second, third = (spot[axis] for axis in AXES[part])
        place = ((core * RING + third) * RING + second) * RING + first
        here = 128 * FIRST[part] + place * PARTS[part] + inner - FIRST[part]
        row = here if row is None else jnp.where(inner >= FIRST[part], here, row)
    return row


class Gather:
    SUBS = (0, -1, 1, 2)
    HOPS = (1, -1, 2)

    def __init__(self, ref, sems, core, spot, lat, lon):
        self.ref = ref
        self.sems = sems
        self.core, self.spot = core, spot
        self.other = (lat + 1 - 2 * core, lon)
        self.makers = []

    def device(self, axis, step):
        spot = dict(self.spot)
        spot[axis] = (spot[axis] + step + RING) % RING
        return (2 * spot["z"] + self.core, RING * spot["y"] + spot["x"])

    def rows(self, part, level, steps, half=None, core=None):
        place = self.core if core is None else core
        for at in (2, 1, 0):
            if at >= level:
                place = place * RING + (self.spot[AXES[part][at]] + steps.get(at, 0) + RING) % RING
        size = PARTS[part] * RING**level
        start = 128 * FIRST[part] + place * size
        if half is not None:
            cut = (size + 1) // 2
            start, size = (start, cut) if half == 0 else (start + cut, size - cut)
        return pl.ds(start, size)

    def copy(self, name, index, rows, device):
        send, recv = self.sems[name]
        return pltpu.make_async_remote_copy(
            src_ref=self.ref.at[rows],
            dst_ref=self.ref.at[rows],
            send_sem=send.at[index],
            recv_sem=recv.at[index],
            device_id=device,
            device_id_type=MESH,
        )

    def go(self, name, index, where, target):
        self.makers.append((name, index, where, target))
        self.make(name, index, where, target).start()

    def make(self, name, index, where, target):
        device = self.other if target is None else self.device(*target)
        return self.copy(name, index, self.rows(*where), device)

    def finish(self):
        for spec in self.makers:
            self.make(*spec).wait_send()

    def take(self, name, index, where):
        self.copy(name, index, self.rows(*where), self.other).wait_recv()

    def start_first(self):
        for n, hop in enumerate(self.HOPS):
            for part in range(3):
                self.go("first", (part, n), (part, 0, {}), (AXES[part][0], hop))

    def wait_first(self):
        for n, hop in enumerate(self.HOPS):
            for part in range(3):
                self.take("first", (part, n), (part, 0, {0: -hop}))

    def start_second(self):
        for kind, step in enumerate((1, -1)):
            for part in range(3):
                self.go("second", (part, kind), (part, 1, {}), (AXES[part][1], step))

    def wait_second(self):
        for kind, step in enumerate((1, -1)):
            for part in range(3):
                self.take("second", (part, kind), (part, 1, {1: -step}))

    def start_second_on(self):
        for kind, step in enumerate((1, -1)):
            for part in range(3):
                self.go(
                    "second", (part, kind + 2), (part, 1, {1: -step}, kind), (AXES[part][1], step)
                )

    def wait_second_on(self):
        for kind, step in enumerate((1, -1)):
            for part in range(3):
                self.take("second", (part, kind + 2), (part, 1, {1: -2 * step}, kind))

    def start_third(self, subs):
        for n in subs:
            for kind, step in enumerate((1, -1)):
                for part in range(3):
                    self.go(
                        "third", (part, n, kind), (part, 1, {1: self.SUBS[n]}), (AXES[part][2], step)
                    )

    def wait_third(self, subs):
        for n in subs:
            for kind, step in enumerate((1, -1)):
                for part in range(3):
                    self.take(
                        "third", (part, n, kind), (part, 1, {1: self.SUBS[n], 2: -step})
                    )

    def start_third_on(self, subs):
        for n in subs:
            step = 1 if n in (0, 2) else -1
            for part in range(3):
                self.go(
                    "on", (part, n), (part, 1, {1: self.SUBS[n], 2: -step}), (AXES[part][2], step)
                )

    def wait_third_on(self, subs):
        for n in subs:
            step = 1 if n in (0, 2) else -1
            for part in range(3):
                self.take("on", (part, n), (part, 1, {1: self.SUBS[n], 2: -2 * step}))

    def sibling_where(self, part, slot, core):
        if slot < 3:
            return (part, 2, {2: (0, -1, 1)[slot]}, None, core)
        return (part, 1, {1: self.SUBS[slot - 3], 2: 2}, None, core)

    def start_sibling(self, slots):
        for slot in slots:
            for part in range(3):
                self.go("core", (part, slot), self.sibling_where(part, slot, self.core), None)

    def wait_sibling(self, slots):
        for slot in slots:
            for part in range(3):
                self.take("core", (part, slot), self.sibling_where(part, slot, 1 - self.core))


def layer_kernel(
    head_ref, ids_ref, mask_ref, gain_ref, mgain_ref, pool_ref,
    tok_hbm, wq_hbm, wk_hbm, wv_hbm, wout_hbm, wup_hbm, wdown_hbm,
    out_ref,
    tok_ref, up_ref, down_ref, left_ref, right_ref, corner_ref,
    wq_ref, wk_ref, wv_ref, wout_ref, wup_ref, wdown_ref,
    every_ref, nb_ref, q_ref, k_ref, v_ref, far_ref, near_ref, high_ref, total_ref, attn_ref,
    rows_ref, idx_ref, bias_ref,
    load_sem, halo_send, halo_recv, *ring_sems,
):
    lat, lon = lax.axis_index("lat"), lax.axis_index("lon")
    lats, lons = 8, 16
    core = lat % 2
    spot = {"x": lon % RING, "y": lon // RING, "z": lat // 2}
    names = ("first", "second", "third", "on", "core")
    sems = {name: (ring_sems[2 * n], ring_sems[2 * n + 1]) for n, name in enumerate(names)}
    gather = Gather(every_ref, sems, core, spot, lat, lon)

    loads = [
        pltpu.make_async_copy(src, dst, load_sem.at[n])
        for n, (src, dst) in enumerate(
            (
                (tok_hbm, tok_ref), (wq_hbm, wq_ref), (wk_hbm, wk_ref), (wv_hbm, wv_ref),
                (wout_hbm, wout_ref), (wup_hbm, wup_ref), (wdown_hbm, wdown_ref),
            )
        )
    ]
    for load in loads:
        load.start()

    def tile(lat_step, lon_step):
        return ((lat + lat_step + lats) % lats, (lon + lon_step + lons) % lons)

    halos = (
        (tok_hbm.at[BLK : 2 * BLK], up_ref, tile(1, 0)),
        (tok_hbm.at[0:BLK], down_ref, tile(-1, 0)),
        (tok_hbm.at[:, COLS - 1], left_ref, tile(0, 1)),
        (tok_hbm.at[:, 0], right_ref, tile(0, -1)),
        (tok_hbm.at[BLK : 2 * BLK, COLS - 1], corner_ref.at[0], tile(1, 1)),
        (tok_hbm.at[BLK : 2 * BLK, 0], corner_ref.at[1], tile(1, -1)),
        (tok_hbm.at[0:BLK, COLS - 1], corner_ref.at[2], tile(-1, 1)),
        (tok_hbm.at[0:BLK, 0], corner_ref.at[3], tile(-1, -1)),
    )
    halo_copies = [
        pltpu.make_async_remote_copy(
            src_ref=src, dst_ref=dst, send_sem=halo_send.at[n], recv_sem=halo_recv.at[n],
            device_id=device, device_id_type=MESH,
        )
        for n, (src, dst, device) in enumerate(halos)
    ]
    partners = [device for _, _, device in halos]
    partners += [gather.device(axis, step) for axis in ("x", "y", "z") for step in (1, -1, 2)]
    partners += [(lat + 1 - 2 * core, lon)]
    barrier = pltpu.get_barrier_semaphore()
    for partner in partners:
        pl.semaphore_signal(barrier, inc=1, device_id=partner, device_id_type=MESH)

    gain = gain_ref[...]
    pool_weight = pool_ref[...]

    ids = ids_ref[...]
    grow, gcol = ids >> 7, ids & 127
    to_lat, to_lon = grow >> 1, gcol >> 3
    to_spot = {"x": to_lon & 3, "y": to_lon >> 2, "z": to_lat >> 1}
    rows_ref[...] = jnp.zeros_like(rows_ref)
    rows_ref[:, :FAR] = summary_row(to_lat & 1, to_spot, (grow & 1) * COLS + (gcol & 7))
    index_load = pltpu.make_async_copy(rows_ref, idx_ref, load_sem.at[7])
    index_load.start()
    slot = lax.broadcasted_iota(jnp.int32, (FAR, FAR * SUMROWS), 0)
    key = lax.broadcasted_iota(jnp.int32, (FAR, FAR * SUMROWS), 1)
    spread = jnp.where(key // SUMROWS == slot, 1.0, 0.0).astype(BF16)
    used = jnp.where(mask_ref[...] > 0, 1.0, 0.0).astype(BF16)
    bias_ref[...] = jnp.where(dot(used, spread) > 0.5, 0.0, NEG)

    pl.semaphore_wait(barrier, len(partners))
    for copy in halo_copies:
        copy.start()
    loads[0].wait()

    def block_of(ref, first, column):
        return jnp.concatenate([ref[first + r, column].astype(F32) for r in range(BLK)], axis=0)

    for part in range(3):
        base = gather.rows(part, 0, {}).start

        def pool_block(n, carry):
            b = n + FIRST[part]
            i, j = b // COLS, b % COLS
            normed = rms(block_of(tok_ref, i * BLK, j), gain)
            nb_ref[i + 1, pl.ds(pl.multiple_of((j + 1) * TOK, TOK), TOK), :] = normed
            every_ref[base + n] = dot(pool_weight, normed).astype(BF16)
            return carry

        lax.fori_loop(0, PARTS[part], pool_block, 0)
    gather.start_first()

    inner = slice(TOK, TOK + ROW)
    loads[1].wait()
    loads[2].wait()
    loads[3].wait()

    def local_qkv(i):
        normed = nb_ref[i + 1, inner, :]
        q_ref[i] = dot(normed, wq_ref[...]).astype(BF16)
        k_ref[i + 1, inner, :] = dot(normed, wk_ref[...]).astype(BF16)
        v_ref[i + 1, inner, :] = dot(normed, wv_ref[...]).astype(BF16)

    local_qkv(0)
    gather.wait_first()
    gather.start_second()
    gather.start_third((0,))
    local_qkv(1)
    gather.wait_second()
    gather.start_second_on()
    gather.start_third((1, 2))

    for copy in halo_copies:
        copy.wait_recv()

    def outer_kv(bi, rows):
        normed = nb_ref[bi, rows, :]
        k_ref[bi, rows, :] = dot(normed, wk_ref[...]).astype(BF16)
        v_ref[bi, rows, :] = dot(normed, wv_ref[...]).astype(BF16)

    last = slice(TOK + ROW, WIDE)
    first = slice(0, TOK)

    def outer_row(bi, ref, corner):
        def put(j, carry):
            rows = pl.ds(pl.multiple_of((j + 1) * TOK, TOK), TOK)
            nb_ref[bi, rows, :] = rms(block_of(ref, 0, j), gain)
            return carry

        lax.fori_loop(0, COLS, put, 0, unroll=2)
        for rows, n in ((first, corner), (last, corner + 1)):
            block = jnp.concatenate([corner_ref[n, r].astype(F32) for r in range(BLK)], axis=0)
            nb_ref[bi, rows, :] = rms(block, gain)
        outer_kv(bi, slice(0, WIDE))

    outer_row(0, up_ref, 0)
    gather.wait_second_on()
    gather.start_third((3,))
    gather.start_sibling((0,))
    gather.wait_third((0,))
    gather.start_third_on((0,))
    outer_row(3, down_ref, 2)
    for i in range(2):
        for ref, rows in ((left_ref, first), (right_ref, last)):
            block = jnp.concatenate([ref[i * BLK + r].astype(F32) for r in range(BLK)], axis=0)
            nb_ref[i + 1, rows, :] = rms(block, gain)
            outer_kv(i + 1, rows)

    lane_head = lax.broadcasted_iota(jnp.int32, (TOK, 256), 1) // TOK

    def stacked_query(i, rows, feats):
        query = q_ref[i, rows, feats]
        zero = jnp.zeros_like(query)
        return jnp.concatenate([jnp.where(lane_head == h, query, zero) for h in range(4)], axis=0)

    def scores(query, keys):
        return lax.dot_general(query, keys, (((1,), (1,)), ((), ())), preferred_element_type=F32)

    def soft_sum(score, values, scales, bias):
        weights, highs, totals = [], [], []
        for h in range(4):
            part = bias(score[h * TOK : (h + 1) * TOK])
            highest = jnp.max(part, axis=-1, keepdims=True)
            expo = jnp.exp2((part - highest) * scales[h])
            highs.append(highest)
            totals.append(jnp.sum(expo, axis=-1, keepdims=True))
            weights.append(expo.astype(BF16))
        full = dot(jnp.concatenate(weights, axis=0), values)
        picked = full[0:TOK]
        high = jnp.broadcast_to(highs[0], (TOK, 256))
        total = jnp.broadcast_to(totals[0], (TOK, 256))
        for h in range(1, 4):
            mine = lane_head == h
            picked = jnp.where(mine, full[h * TOK : (h + 1) * TOK], picked)
            high = jnp.where(mine, highs[h], high)
            total = jnp.where(mine, totals[h], total)
        return picked, high, total

    def near_block(b, carry):
        i, j = b // COLS, b % COLS
        start = pl.multiple_of(j * TOK, TOK)
        rows = pl.ds(start, TOK)
        around = pl.ds(start, 3 * TOK)
        inside = jnp.where(i == 0, lat > 0, lat < lats - 1)
        edge = jnp.where(inside, jnp.float32(0.0), jnp.float32(NEG))
        for g in range(2):
            feats = slice(g * 256, (g + 1) * 256)
            keys = jnp.concatenate([k_ref[d, around, feats] for d in (1, 2, 3 * i)], axis=0)
            values = jnp.concatenate([v_ref[d, around, feats] for d in (1, 2, 3 * i)], axis=0)
            score = scores(stacked_query(i, rows, feats), keys)
            near_ref[i, rows, feats], high_ref[i, rows, feats], total_ref[i, rows, feats] = soft_sum(
                score, values, [head_ref[0, g * 4 + h] * SCALE for h in range(4)],
                lambda part: jnp.concatenate([part[:, :384], part[:, 384:] + edge], axis=1),
            )
        return carry

    def pump_a():
        gather.wait_third((1, 2))
        gather.start_third_on((1, 2))

    def pump_b():
        gather.wait_third((3,))
        gather.start_third_on((3,))
        gather.start_sibling((1, 2))

    def pump_c():
        gather.wait_third_on((0, 1))
        gather.start_sibling((3, 4))

    def pump_d():
        gather.wait_third_on((2, 3))
        gather.start_sibling((5, 6))

    pumps = ((PUMP_A, pump_a), (PUMP_B, pump_b), (PUMP_C, pump_c), (PUMP_D, pump_d))

    def near_step(b, carry):
        for when, pump in pumps:
            pl.when(b == when)(pump)
        return near_block(b, carry)

    lax.fori_loop(0, 16, near_step, 0)
    gather.wait_sibling(range(7))
    index_load.wait()

    def far_block(b, carry):
        i, j = b // COLS, b % COLS
        rows = pl.ds(pl.multiple_of(j * TOK, TOK), TOK)
        for s in range(FAR):
            far_ref[s * SUMROWS : (s + 1) * SUMROWS, :] = every_ref[idx_ref[b, s]]
        far = far_ref[...]
        keys = dot(far, wk_ref[...]).astype(BF16)
        values = dot(far, wv_ref[...]).astype(BF16)
        bias = bias_ref[pl.ds(b, 1), :]
        for g in range(2):
            feats = slice(g * 256, (g + 1) * 256)
            score = scores(stacked_query(i, rows, feats), keys[:, feats])
            scales = [head_ref[0, g * 4 + h] * SCALE for h in range(4)]
            far_sum, far_high, far_total = soft_sum(
                score, values[:, feats], scales, lambda part: part + bias
            )
            scale = jnp.full((1, 256), scales[0], F32)
            for h in range(1, 4):
                scale = jnp.where(lane_head[:1] == h, scales[h], scale)
            near_high = high_ref[i, rows, feats]
            high = jnp.maximum(near_high, far_high)
            near_part = jnp.exp2((near_high - high) * scale)
            far_part = jnp.exp2((far_high - high) * scale)
            total = total_ref[i, rows, feats] * near_part + far_total * far_part
            mixed = near_ref[i, rows, feats] * near_part + far_sum * far_part
            attn_ref[i, rows, feats] = (mixed / total).astype(BF16)
        return carry

    lax.fori_loop(0, 16, far_block, 0)

    for load in loads[4:]:
        load.wait()
    mgain = mgain_ref[...]

    def feed_forward(t, carry):
        i, half = t // 2, t % 2
        rows = pl.ds(pl.multiple_of(half * 256, 256), 256)
        token = jnp.concatenate(
            [block_of(tok_ref, i * BLK, half * 4 + j) for j in range(4)], axis=0
        )
        mixed = (token + dot(attn_ref[i, rows, :], wout_ref[...])).astype(BF16)
        wide = mixed.astype(F32)
        normed = rms(wide, mgain)
        acc = wide
        for f in range(4):
            part = slice(f * 512, (f + 1) * 512)
            hidden = jax.nn.gelu(dot(normed, wup_ref[:, part]), approximate=True).astype(BF16)
            acc = acc + dot(hidden, wdown_ref[part, :])
        for r in range(BLK):
            row = jnp.concatenate(
                [acc[j * TOK + r * BLK : j * TOK + (r + 1) * BLK] for j in range(4)], axis=0
            )
            out_ref[i * BLK + r, pl.ds(pl.multiple_of(half * 32, 32), 32), :] = row.astype(BF16)
        return carry

    lax.fori_loop(0, 4, feed_forward, 0)
    for copy in halo_copies:
        copy.wait_send()
    gather.finish()


def layer_call(head_scale, ids, mask, gain, mgain, pool_weight, tokens, weights):
    rows, cols, feature = tokens.shape
    vmem = pl.BlockSpec(memory_space=pltpu.VMEM)
    smem = pl.BlockSpec(memory_space=pltpu.SMEM)
    hbm = pl.BlockSpec(memory_space=pl.ANY)
    half = (BLK, COLS, BLK, feature)
    dma = pltpu.SemaphoreType.DMA
    return pl.pallas_call(
        layer_kernel,
        out_shape=jax.ShapeDtypeStruct(tokens.shape, BF16),
        in_specs=[smem] + [vmem] * 5 + [hbm] * 7,
        out_specs=vmem,
        scratch_shapes=[
            pltpu.VMEM((2 * BLK, COLS, BLK, feature), BF16),
            pltpu.VMEM(half, BF16),
            pltpu.VMEM(half, BF16),
            pltpu.VMEM((2 * BLK, BLK, feature), BF16),
            pltpu.VMEM((2 * BLK, BLK, feature), BF16),
            pltpu.VMEM((4, BLK, BLK, feature), BF16),
        ]
        + [pltpu.VMEM(weight.shape, BF16) for weight in weights]
        + [
            pltpu.VMEM((2048, SUMROWS, feature), BF16),
            pltpu.VMEM((4, WIDE, feature), BF16),
            pltpu.VMEM((2, ROW, feature), BF16),
            pltpu.VMEM((4, WIDE, feature), BF16),
            pltpu.VMEM((4, WIDE, feature), BF16),
            pltpu.VMEM((FAR * SUMROWS, feature), BF16),
            pltpu.VMEM((2, ROW, feature), F32),
            pltpu.VMEM((2, ROW, feature), F32),
            pltpu.VMEM((2, ROW, feature), F32),
            pltpu.VMEM((2, ROW, feature), BF16),
            pltpu.VMEM((2 * COLS, 128), jnp.int32),
            pltpu.SMEM((2 * COLS, 128), jnp.int32),
            pltpu.VMEM((2 * COLS, FAR * SUMROWS), F32),
            dma((8,)), dma((8,)), dma((8,)),
        ]
        + [dma(shape) for shape in ((3, 3), (3, 4), (3, 4, 2), (3, 4), (3, 7)) for _ in range(2)],
        compiler_params=pltpu.CompilerParams(
            vmem_limit_bytes=60 << 20, collective_id=0, has_side_effects=True
        ),
        name="layer",
    )(
        head_scale, ids, mask, gain.reshape(1, feature), mgain.reshape(1, feature), pool_weight,
        tokens.reshape(rows, COLS, BLK, feature), *weights,
    )


def local(
    tokens, norm_gain, w_query, w_key, w_value, w_out, pool_weight, head_scale,
    far_ids, far_mask, mlp_gain, w_up, w_down,
):
    return layer_call(
        head_scale.reshape(1, -1), far_ids.reshape(-1, FAR), far_mask.reshape(-1, FAR),
        norm_gain, mlp_gain, pool_weight, tokens,
        (w_query, w_key, w_value, w_out, w_up, w_down),
    )


def solution(mesh):
    return jax.shard_map(
        local,
        mesh=mesh,
        in_specs=(
            P("lat", "lon", None),
            P(), P(), P(), P(), P(), P(), P(),
            P("lat", "lon", None),
            P("lat", "lon", None),
            P(), P(), P(),
        ),
        out_specs=P("lat", "lon", None),
        check_vma=False,
    )
```

```python
import math

import jax
import jax.numpy as jnp
from jax import lax
from jax.experimental import pallas as pl
from jax.experimental.pallas import tpu as pltpu
from jax.sharding import PartitionSpec as P

BLK = 8
TOK = BLK * BLK
SUMROWS = 4
FAR = 48
EPS = 1e-06
NEG = -1e30
SCALE = 1.4426950408889634 / math.sqrt(64)
PUMP_S, PUMP_A, PUMP_B, PUMP_C, PUMP_D = 1, 4, 7, 10, 13
F32 = jnp.float32
BF16 = jnp.bfloat16
MESH = pl.DeviceIdType.MESH

RING = 4
PARTS = (4, 5, 7)
FIRST = (0, 4, 9)
AXES = (("x", "y", "z"), ("y", "z", "x"), ("z", "x", "y"))
COLS = 8
WIDE = (COLS + 2) * TOK
ROW = COLS * TOK


def rms(wide, gain):
    mean_square = jnp.mean(wide * wide, axis=-1, keepdims=True)
    return (wide * lax.rsqrt(mean_square + EPS) * gain).astype(BF16)


def dot(a, b):
    return jnp.dot(a, b, preferred_element_type=F32)


def summary_row(core, spot, inner):
    row = None
    for part in range(3):
        first, second, third = (spot[axis] for axis in AXES[part])
        place = ((core * RING + third) * RING + second) * RING + first
        here = 128 * FIRST[part] + place * PARTS[part] + inner - FIRST[part]
        row = here if row is None else jnp.where(inner >= FIRST[part], here, row)
    return row


class Gather:
    SUBS = (0, -1, 1, 2)
    HOPS = (1, -1, 2)

    def __init__(self, ref, sems, core, spot, lat, lon):
        self.ref = ref
        self.sems = sems
        self.core, self.spot = core, spot
        self.other = (lat + 1 - 2 * core, lon)
        self.makers = []

    def device(self, axis, step):
        spot = dict(self.spot)
        spot[axis] = (spot[axis] + step + RING) % RING
        return (2 * spot["z"] + self.core, RING * spot["y"] + spot["x"])

    def rows(self, part, level, steps, half=None, core=None):
        place = self.core if core is None else core
        for at in (2, 1, 0):
            if at >= level:
                place = place * RING + (self.spot[AXES[part][at]] + steps.get(at, 0) + RING) % RING
        size = PARTS[part] * RING**level
        start = 128 * FIRST[part] + place * size
        if half is not None:
            cut = (size + 1) // 2
            start, size = (start, cut) if half == 0 else (start + cut, size - cut)
        return pl.ds(start, size)

    def copy(self, name, index, rows, device):
        send, recv = self.sems[name]
        return pltpu.make_async_remote_copy(
            src_ref=self.ref.at[rows],
            dst_ref=self.ref.at[rows],
            send_sem=send.at[index],
            recv_sem=recv.at[index],
            device_id=device,
            device_id_type=MESH,
        )

    def go(self, name, index, where, target):
        self.makers.append((name, index, where, target))
        self.make(name, index, where, target).start()

    def make(self, name, index, where, target):
        device = self.other if target is None else self.device(*target)
        return self.copy(name, index, self.rows(*where), device)

    def finish(self):
        for spec in self.makers:
            self.make(*spec).wait_send()

    def take(self, name, index, where):
        self.copy(name, index, self.rows(*where), self.other).wait_recv()

    def start_first(self):
        for n, hop in enumerate(self.HOPS):
            for part in range(3):
                self.go("first", (part, n), (part, 0, {}), (AXES[part][0], hop))

    def wait_first(self):
        for n, hop in enumerate(self.HOPS):
            for part in range(3):
                self.take("first", (part, n), (part, 0, {0: -hop}))

    def start_second(self):
        for kind, step in enumerate((1, -1)):
            for part in range(3):
                self.go("second", (part, kind), (part, 1, {}), (AXES[part][1], step))

    def wait_second(self):
        for kind, step in enumerate((1, -1)):
            for part in range(3):
                self.take("second", (part, kind), (part, 1, {1: -step}))

    def start_second_on(self):
        for kind, step in enumerate((1, -1)):
            for part in range(3):
                self.go(
                    "second", (part, kind + 2), (part, 1, {1: -step}, kind), (AXES[part][1], step)
                )

    def wait_second_on(self):
        for kind, step in enumerate((1, -1)):
            for part in range(3):
                self.take("second", (part, kind + 2), (part, 1, {1: -2 * step}, kind))

    def start_third(self, subs):
        for n in subs:
            for kind, step in enumerate((1, -1)):
                for part in range(3):
                    self.go(
                        "third", (part, n, kind), (part, 1, {1: self.SUBS[n]}), (AXES[part][2], step)
                    )

    def wait_third(self, subs):
        for n in subs:
            for kind, step in enumerate((1, -1)):
                for part in range(3):
                    self.take(
                        "third", (part, n, kind), (part, 1, {1: self.SUBS[n], 2: -step})
                    )

    def start_third_on(self, subs):
        for n in subs:
            step = 1 if n in (0, 2) else -1
            for part in range(3):
                self.go(
                    "on", (part, n), (part, 1, {1: self.SUBS[n], 2: -step}), (AXES[part][2], step)
                )

    def wait_third_on(self, subs):
        for n in subs:
            step = 1 if n in (0, 2) else -1
            for part in range(3):
                self.take("on", (part, n), (part, 1, {1: self.SUBS[n], 2: -2 * step}))

    def sibling_where(self, part, slot, core):
        if slot < 3:
            return (part, 2, {2: (0, -1, 1)[slot]}, None, core)
        return (part, 1, {1: self.SUBS[slot - 3], 2: 2}, None, core)

    def start_sibling(self, slots):
        for slot in slots:
            for part in range(3):
                self.go("core", (part, slot), self.sibling_where(part, slot, self.core), None)

    def wait_sibling(self, slots):
        for slot in slots:
            for part in range(3):
                self.take("core", (part, slot), self.sibling_where(part, slot, 1 - self.core))


def layer_kernel(
    head_ref, ids_ref, mask_ref, gain_ref, mgain_ref, pool_ref,
    tok_hbm, wq_hbm, wk_hbm, wv_hbm, wout_hbm, wup_hbm, wdown_hbm,
    out_ref,
    tok_ref, up_ref, down_ref, left_ref, right_ref, corner_ref,
    wq_ref, wk_ref, wv_ref, wout_ref, wup_ref, wdown_ref,
    every_ref, nb_ref, q_ref, k_ref, v_ref, far_ref, near_ref, high_ref, total_ref, attn_ref,
    rows_ref, idx_ref, bias_ref,
    load_sem, halo_send, halo_recv, *ring_sems,
):
    lat, lon = lax.axis_index("lat"), lax.axis_index("lon")
    lats, lons = 8, 16
    core = lat % 2
    spot = {"x": lon % RING, "y": lon // RING, "z": lat // 2}
    names = ("first", "second", "third", "on", "core")
    sems = {name: (ring_sems[2 * n], ring_sems[2 * n + 1]) for n, name in enumerate(names)}
    gather = Gather(every_ref, sems, core, spot, lat, lon)

    loads = [
        pltpu.make_async_copy(src, dst, load_sem.at[n])
        for n, (src, dst) in enumerate(
            (
                (tok_hbm, tok_ref), (wq_hbm, wq_ref), (wk_hbm, wk_ref), (wv_hbm, wv_ref),
                (wout_hbm, wout_ref), (wup_hbm, wup_ref), (wdown_hbm, wdown_ref),
            )
        )
    ]
    for load in loads:
        load.start()

    def tile(lat_step, lon_step):
        return ((lat + lat_step + lats) % lats, (lon + lon_step + lons) % lons)

    halos = (
        (tok_hbm.at[BLK : 2 * BLK], up_ref, tile(1, 0)),
        (tok_hbm.at[0:BLK], down_ref, tile(-1, 0)),
        (tok_hbm.at[:, COLS - 1], left_ref, tile(0, 1)),
        (tok_hbm.at[:, 0], right_ref, tile(0, -1)),
        (tok_hbm.at[BLK : 2 * BLK, COLS - 1], corner_ref.at[0], tile(1, 1)),
        (tok_hbm.at[BLK : 2 * BLK, 0], corner_ref.at[1], tile(1, -1)),
        (tok_hbm.at[0:BLK, COLS - 1], corner_ref.at[2], tile(-1, 1)),
        (tok_hbm.at[0:BLK, 0], corner_ref.at[3], tile(-1, -1)),
    )
    halo_copies = [
        pltpu.make_async_remote_copy(
            src_ref=src, dst_ref=dst, send_sem=halo_send.at[n], recv_sem=halo_recv.at[n],
            device_id=device, device_id_type=MESH,
        )
        for n, (src, dst, device) in enumerate(halos)
    ]
    partners = [device for _, _, device in halos]
    partners += [gather.device(axis, step) for axis in ("x", "y", "z") for step in (1, -1, 2)]
    partners += [(lat + 1 - 2 * core, lon)]
    barrier = pltpu.get_barrier_semaphore()
    for partner in partners:
        pl.semaphore_signal(barrier, inc=1, device_id=partner, device_id_type=MESH)

    gain = gain_ref[...]
    pool_weight = pool_ref[...]

    ids = ids_ref[...]
    grow, gcol = ids >> 7, ids & 127
    to_lat, to_lon = grow >> 1, gcol >> 3
    to_spot = {"x": to_lon & 3, "y": to_lon >> 2, "z": to_lat >> 1}
    rows_ref[...] = jnp.zeros_like(rows_ref)
    rows_ref[:, :FAR] = summary_row(to_lat & 1, to_spot, (grow & 1) * COLS + (gcol & 7))
    index_load = pltpu.make_async_copy(rows_ref, idx_ref, load_sem.at[7])
    index_load.start()
    slot = lax.broadcasted_iota(jnp.int32, (FAR, FAR * SUMROWS), 0)
    key = lax.broadcasted_iota(jnp.int32, (FAR, FAR * SUMROWS), 1)
    spread = jnp.where(key // SUMROWS == slot, 1.0, 0.0).astype(BF16)
    used = jnp.where(mask_ref[...] > 0, 1.0, 0.0).astype(BF16)
    bias_ref[...] = jnp.where(dot(used, spread) > 0.5, 0.0, NEG)

    loads[0].wait()

    def block_of(ref, first, column):
        return jnp.concatenate([ref[first + r, column].astype(F32) for r in range(BLK)], axis=0)

    for part in range(3):
        base = gather.rows(part, 0, {}).start

        def pool_block(n, carry):
            b = n + FIRST[part]
            i, j = b // COLS, b % COLS
            normed = rms(block_of(tok_ref, i * BLK, j), gain)
            nb_ref[i + 1, pl.ds(pl.multiple_of((j + 1) * TOK, TOK), TOK), :] = normed
            every_ref[base + n] = dot(pool_weight, normed).astype(BF16)
            return carry

        lax.fori_loop(0, PARTS[part], pool_block, 0)
    pl.semaphore_wait(barrier, len(partners))
    gather.start_first()
    for copy in halo_copies:
        copy.start()

    inner = slice(TOK, TOK + ROW)
    loads[1].wait()
    loads[2].wait()
    loads[3].wait()

    def local_qkv(i):
        normed = nb_ref[i + 1, inner, :]
        q_ref[i] = dot(normed, wq_ref[...]).astype(BF16)
        k_ref[i + 1, inner, :] = dot(normed, wk_ref[...]).astype(BF16)
        v_ref[i + 1, inner, :] = dot(normed, wv_ref[...]).astype(BF16)

    local_qkv(0)
    gather.wait_first()
    gather.start_second()
    gather.start_third((0,))
    local_qkv(1)

    for copy in halo_copies:
        copy.wait_recv()

    def outer_kv(bi, rows):
        normed = nb_ref[bi, rows, :]
        k_ref[bi, rows, :] = dot(normed, wk_ref[...]).astype(BF16)
        v_ref[bi, rows, :] = dot(normed, wv_ref[...]).astype(BF16)

    last = slice(TOK + ROW, WIDE)
    first = slice(0, TOK)

    def outer_row(bi, ref, corner):
        def put(j, carry):
            rows = pl.ds(pl.multiple_of((j + 1) * TOK, TOK), TOK)
            nb_ref[bi, rows, :] = rms(block_of(ref, 0, j), gain)
            return carry

        lax.fori_loop(0, COLS, put, 0, unroll=2)
        for rows, n in ((first, corner), (last, corner + 1)):
            block = jnp.concatenate([corner_ref[n, r].astype(F32) for r in range(BLK)], axis=0)
            nb_ref[bi, rows, :] = rms(block, gain)
        outer_kv(bi, slice(0, WIDE))

    outer_row(0, up_ref, 0)
    gather.wait_second()
    gather.start_second_on()
    gather.start_third((1, 2))
    outer_row(3, down_ref, 2)
    for i in range(2):
        for ref, rows in ((left_ref, first), (right_ref, last)):
            block = jnp.concatenate([ref[i * BLK + r].astype(F32) for r in range(BLK)], axis=0)
            nb_ref[i + 1, rows, :] = rms(block, gain)
            outer_kv(i + 1, rows)

    lane_head = lax.broadcasted_iota(jnp.int32, (TOK, 256), 1) // TOK

    def stacked_query(i, rows, feats):
        query = q_ref[i, rows, feats]
        zero = jnp.zeros_like(query)
        return jnp.concatenate([jnp.where(lane_head == h, query, zero) for h in range(4)], axis=0)

    def scores(query, keys):
        return lax.dot_general(query, keys, (((1,), (1,)), ((), ())), preferred_element_type=F32)

    def soft_sum(score, values, scales, bias):
        weights, highs, totals = [], [], []
        for h in range(4):
            part = bias(score[h * TOK : (h + 1) * TOK])
            highest = jnp.max(part, axis=-1, keepdims=True)
            expo = jnp.exp2((part - highest) * scales[h])
            highs.append(highest)
            totals.append(jnp.sum(expo, axis=-1, keepdims=True))
            weights.append(expo.astype(BF16))
        full = dot(jnp.concatenate(weights, axis=0), values)
        picked = full[0:TOK]
        high = jnp.broadcast_to(highs[0], (TOK, 256))
        total = jnp.broadcast_to(totals[0], (TOK, 256))
        for h in range(1, 4):
            mine = lane_head == h
            picked = jnp.where(mine, full[h * TOK : (h + 1) * TOK], picked)
            high = jnp.where(mine, highs[h], high)
            total = jnp.where(mine, totals[h], total)
        return picked, high, total

    def near_block(b, carry):
        i, j = b // COLS, b % COLS
        start = pl.multiple_of(j * TOK, TOK)
        rows = pl.ds(start, TOK)
        around = pl.ds(start, 3 * TOK)
        inside = jnp.where(i == 0, lat > 0, lat < lats - 1)
        edge = jnp.where(inside, jnp.float32(0.0), jnp.float32(NEG))
        for g in range(2):
            feats = slice(g * 256, (g + 1) * 256)
            keys = jnp.concatenate([k_ref[d, around, feats] for d in (1, 2, 3 * i)], axis=0)
            values = jnp.concatenate([v_ref[d, around, feats] for d in (1, 2, 3 * i)], axis=0)
            score = scores(stacked_query(i, rows, feats), keys)
            near_ref[i, rows, feats], high_ref[i, rows, feats], total_ref[i, rows, feats] = soft_sum(
                score, values, [head_ref[0, g * 4 + h] * SCALE for h in range(4)],
                lambda part: jnp.concatenate([part[:, :384], part[:, 384:] + edge], axis=1),
            )
        return carry

    def pump_s():
        gather.wait_second_on()
        gather.start_third((3,))
        gather.start_sibling((0,))
        gather.wait_third((0,))
        gather.start_third_on((0,))

    def pump_a():
        gather.wait_third((1, 2))
        gather.start_third_on((1, 2))

    def pump_b():
        gather.wait_third((3,))
        gather.start_third_on((3,))
        gather.start_sibling((1, 2))

    def pump_c():
        gather.wait_third_on((0, 1))
        gather.start_sibling((3, 4))

    def pump_d():
        gather.wait_third_on((2, 3))
        gather.start_sibling((5, 6))

    pumps = ((PUMP_S, pump_s), (PUMP_A, pump_a), (PUMP_B, pump_b), (PUMP_C, pump_c), (PUMP_D, pump_d))

    def near_step(b, carry):
        for when, pump in pumps:
            pl.when(b == when)(pump)
        return near_block(b, carry)

    lax.fori_loop(0, 16, near_step, 0)
    gather.wait_sibling(range(7))
    index_load.wait()

    def far_block(b, carry):
        i, j = b // COLS, b % COLS
        rows = pl.ds(pl.multiple_of(j * TOK, TOK), TOK)
        for s in range(FAR):
            far_ref[s * SUMROWS : (s + 1) * SUMROWS, :] = every_ref[idx_ref[b, s]]
        far = far_ref[...]
        keys = dot(far, wk_ref[...]).astype(BF16)
        values = dot(far, wv_ref[...]).astype(BF16)
        bias = bias_ref[pl.ds(b, 1), :]
        for g in range(2):
            feats = slice(g * 256, (g + 1) * 256)
            score = scores(stacked_query(i, rows, feats), keys[:, feats])
            scales = [head_ref[0, g * 4 + h] * SCALE for h in range(4)]
            far_sum, far_high, far_total = soft_sum(
                score, values[:, feats], scales, lambda part: part + bias
            )
            scale = jnp.full((1, 256), scales[0], F32)
            for h in range(1, 4):
                scale = jnp.where(lane_head[:1] == h, scales[h], scale)
            near_high = high_ref[i, rows, feats]
            high = jnp.maximum(near_high, far_high)
            near_part = jnp.exp2((near_high - high) * scale)
            far_part = jnp.exp2((far_high - high) * scale)
            total = total_ref[i, rows, feats] * near_part + far_total * far_part
            mixed = near_ref[i, rows, feats] * near_part + far_sum * far_part
            attn_ref[i, rows, feats] = (mixed / total).astype(BF16)
        return carry

    lax.fori_loop(0, 16, far_block, 0)

    for load in loads[4:]:
        load.wait()
    mgain = mgain_ref[...]

    def feed_forward(t, carry):
        i, half = t // 2, t % 2
        rows = pl.ds(pl.multiple_of(half * 256, 256), 256)
        token = jnp.concatenate(
            [block_of(tok_ref, i * BLK, half * 4 + j) for j in range(4)], axis=0
        )
        mixed = (token + dot(attn_ref[i, rows, :], wout_ref[...])).astype(BF16)
        wide = mixed.astype(F32)
        normed = rms(wide, mgain)
        acc = wide
        for f in range(4):
            part = slice(f * 512, (f + 1) * 512)
            hidden = jax.nn.gelu(dot(normed, wup_ref[:, part]), approximate=True).astype(BF16)
            acc = acc + dot(hidden, wdown_ref[part, :])
        for r in range(BLK):
            row = jnp.concatenate(
                [acc[j * TOK + r * BLK : j * TOK + (r + 1) * BLK] for j in range(4)], axis=0
            )
            out_ref[i * BLK + r, pl.ds(pl.multiple_of(half * 32, 32), 32), :] = row.astype(BF16)
        return carry

    lax.fori_loop(0, 4, feed_forward, 0)
    for copy in halo_copies:
        copy.wait_send()
    gather.finish()


def layer_call(head_scale, ids, mask, gain, mgain, pool_weight, tokens, weights):
    rows, cols, feature = tokens.shape
    vmem = pl.BlockSpec(memory_space=pltpu.VMEM)
    smem = pl.BlockSpec(memory_space=pltpu.SMEM)
    hbm = pl.BlockSpec(memory_space=pl.ANY)
    half = (BLK, COLS, BLK, feature)
    dma = pltpu.SemaphoreType.DMA
    return pl.pallas_call(
        layer_kernel,
        out_shape=jax.ShapeDtypeStruct(tokens.shape, BF16),
        in_specs=[smem] + [vmem] * 5 + [hbm] * 7,
        out_specs=vmem,
        scratch_shapes=[
            pltpu.VMEM((2 * BLK, COLS, BLK, feature), BF16),
            pltpu.VMEM(half, BF16),
            pltpu.VMEM(half, BF16),
            pltpu.VMEM((2 * BLK, BLK, feature), BF16),
            pltpu.VMEM((2 * BLK, BLK, feature), BF16),
            pltpu.VMEM((4, BLK, BLK, feature), BF16),
        ]
        + [pltpu.VMEM(weight.shape, BF16) for weight in weights]
        + [
            pltpu.VMEM((2048, SUMROWS, feature), BF16),
            pltpu.VMEM((4, WIDE, feature), BF16),
            pltpu.VMEM((2, ROW, feature), BF16),
            pltpu.VMEM((4, WIDE, feature), BF16),
            pltpu.VMEM((4, WIDE, feature), BF16),
            pltpu.VMEM((FAR * SUMROWS, feature), BF16),
            pltpu.VMEM((2, ROW, feature), F32),
            pltpu.VMEM((2, ROW, feature), F32),
            pltpu.VMEM((2, ROW, feature), F32),
            pltpu.VMEM((2, ROW, feature), BF16),
            pltpu.VMEM((2 * COLS, 128), jnp.int32),
            pltpu.SMEM((2 * COLS, 128), jnp.int32),
            pltpu.VMEM((2 * COLS, FAR * SUMROWS), F32),
            dma((8,)), dma((8,)), dma((8,)),
        ]
        + [dma(shape) for shape in ((3, 3), (3, 4), (3, 4, 2), (3, 4), (3, 7)) for _ in range(2)],
        compiler_params=pltpu.CompilerParams(
            vmem_limit_bytes=60 << 20, collective_id=0, has_side_effects=True
        ),
        name="layer",
    )(
        head_scale, ids, mask, gain.reshape(1, feature), mgain.reshape(1, feature), pool_weight,
        tokens.reshape(rows, COLS, BLK, feature), *weights,
    )


def local(
    tokens, norm_gain, w_query, w_key, w_value, w_out, pool_weight, head_scale,
    far_ids, far_mask, mlp_gain, w_up, w_down,
):
    return layer_call(
        head_scale.reshape(1, -1), far_ids.reshape(-1, FAR), far_mask.reshape(-1, FAR),
        norm_gain, mlp_gain, pool_weight, tokens,
        (w_query, w_key, w_value, w_out, w_up, w_down),
    )


def solution(mesh):
    return jax.shard_map(
        local,
        mesh=mesh,
        in_specs=(
            P("lat", "lon", None),
            P(), P(), P(), P(), P(), P(), P(),
            P("lat", "lon", None),
            P("lat", "lon", None),
            P(), P(), P(),
        ),
        out_specs=P("lat", "lon", None),
        check_vma=False,
    )
```

```python
import math

import jax
import jax.numpy as jnp
from jax import lax
from jax.experimental import pallas as pl
from jax.experimental.pallas import tpu as pltpu
from jax.sharding import PartitionSpec as P

BLK = 8
TOK = BLK * BLK
SUMROWS = 4
FAR = 48
EPS = 1e-06
NEG = -1e30
SCALE = 1.4426950408889634 / math.sqrt(64)
PUMP_S, PUMP_A, PUMP_B, PUMP_C, PUMP_D = 2, 6, 9, 12, 14
F32 = jnp.float32
BF16 = jnp.bfloat16
MESH = pl.DeviceIdType.MESH

RING = 4
PARTS = (4, 5, 7)
FIRST = (0, 4, 9)
AXES = (("x", "y", "z"), ("y", "z", "x"), ("z", "x", "y"))
COLS = 8
WIDE = (COLS + 2) * TOK
ROW = COLS * TOK


def rms(wide, gain):
    mean_square = jnp.mean(wide * wide, axis=-1, keepdims=True)
    return (wide * lax.rsqrt(mean_square + EPS) * gain).astype(BF16)


def dot(a, b):
    return jnp.dot(a, b, preferred_element_type=F32)


def summary_row(core, spot, inner):
    row = None
    for part in range(3):
        first, second, third = (spot[axis] for axis in AXES[part])
        place = ((core * RING + third) * RING + second) * RING + first
        here = 128 * FIRST[part] + place * PARTS[part] + inner - FIRST[part]
        row = here if row is None else jnp.where(inner >= FIRST[part], here, row)
    return row


class Gather:
    SUBS = (0, -1, 1, 2)
    HOPS = (1, -1, 2)

    def __init__(self, ref, sems, core, spot, lat, lon):
        self.ref = ref
        self.sems = sems
        self.core, self.spot = core, spot
        self.other = (lat + 1 - 2 * core, lon)
        self.makers = []

    def device(self, axis, step):
        spot = dict(self.spot)
        spot[axis] = (spot[axis] + step + RING) % RING
        return (2 * spot["z"] + self.core, RING * spot["y"] + spot["x"])

    def rows(self, part, level, steps, half=None, core=None):
        place = self.core if core is None else core
        for at in (2, 1, 0):
            if at >= level:
                place = place * RING + (self.spot[AXES[part][at]] + steps.get(at, 0) + RING) % RING
        size = PARTS[part] * RING**level
        start = 128 * FIRST[part] + place * size
        if half is not None:
            cut = (size + 1) // 2
            start, size = (start, cut) if half == 0 else (start + cut, size - cut)
        return pl.ds(start, size)

    def copy(self, name, index, rows, device):
        send, recv = self.sems[name]
        return pltpu.make_async_remote_copy(
            src_ref=self.ref.at[rows],
            dst_ref=self.ref.at[rows],
            send_sem=send.at[index],
            recv_sem=recv.at[index],
            device_id=device,
            device_id_type=MESH,
        )

    def go(self, name, index, where, target):
        self.makers.append((name, index, where, target))
        self.make(name, index, where, target).start()

    def make(self, name, index, where, target):
        device = self.other if target is None else self.device(*target)
        return self.copy(name, index, self.rows(*where), device)

    def finish(self):
        for spec in self.makers:
            self.make(*spec).wait_send()

    def take(self, name, index, where):
        self.copy(name, index, self.rows(*where), self.other).wait_recv()

    def start_first(self):
        for n, hop in enumerate(self.HOPS):
            for part in range(3):
                self.go("first", (part, n), (part, 0, {}), (AXES[part][0], hop))

    def wait_first(self):
        for n, hop in enumerate(self.HOPS):
            for part in range(3):
                self.take("first", (part, n), (part, 0, {0: -hop}))

    def start_second(self):
        for kind, step in enumerate((1, -1)):
            for part in range(3):
                self.go("second", (part, kind), (part, 1, {}), (AXES[part][1], step))

    def wait_second(self):
        for kind, step in enumerate((1, -1)):
            for part in range(3):
                self.take("second", (part, kind), (part, 1, {1: -step}))

    def start_second_on(self):
        for kind, step in enumerate((1, -1)):
            for part in range(3):
                self.go(
                    "second", (part, kind + 2), (part, 1, {1: -step}, kind), (AXES[part][1], step)
                )

    def wait_second_on(self):
        for kind, step in enumerate((1, -1)):
            for part in range(3):
                self.take("second", (part, kind + 2), (part, 1, {1: -2 * step}, kind))

    def start_third(self, subs):
        for n in subs:
            for kind, step in enumerate((1, -1)):
                for part in range(3):
                    self.go(
                        "third", (part, n, kind), (part, 1, {1: self.SUBS[n]}), (AXES[part][2], step)
                    )

    def wait_third(self, subs):
        for n in subs:
            for kind, step in enumerate((1, -1)):
                for part in range(3):
                    self.take(
                        "third", (part, n, kind), (part, 1, {1: self.SUBS[n], 2: -step})
                    )

    def start_third_on(self, subs):
        for n in subs:
            step = 1 if n in (0, 2) else -1
            for part in range(3):
                self.go(
                    "on", (part, n), (part, 1, {1: self.SUBS[n], 2: -step}), (AXES[part][2], step)
                )

    def wait_third_on(self, subs):
        for n in subs:
            step = 1 if n in (0, 2) else -1
            for part in range(3):
                self.take("on", (part, n), (part, 1, {1: self.SUBS[n], 2: -2 * step}))

    def sibling_where(self, part, slot, core):
        if slot < 3:
            return (part, 2, {2: (0, -1, 1)[slot]}, None, core)
        return (part, 1, {1: self.SUBS[slot - 3], 2: 2}, None, core)

    def start_sibling(self, slots):
        for slot in slots:
            for part in range(3):
                self.go("core", (part, slot), self.sibling_where(part, slot, self.core), None)

    def wait_sibling(self, slots):
        for slot in slots:
            for part in range(3):
                self.take("core", (part, slot), self.sibling_where(part, slot, 1 - self.core))


def layer_kernel(
    head_ref, ids_ref, mask_ref, gain_ref, mgain_ref, pool_ref,
    tok_hbm, wq_hbm, wk_hbm, wv_hbm, wout_hbm, wup_hbm, wdown_hbm,
    out_ref,
    tok_ref, up_ref, down_ref, left_ref, right_ref, corner_ref,
    wq_ref, wk_ref, wv_ref, wout_ref, wup_ref, wdown_ref,
    every_ref, nb_ref, q_ref, k_ref, v_ref, far_ref, near_ref, high_ref, total_ref, attn_ref,
    rows_ref, idx_ref, bias_ref,
    load_sem, halo_send, halo_recv, *ring_sems,
):
    lat, lon = lax.axis_index("lat"), lax.axis_index("lon")
    lats, lons = 8, 16
    core = lat % 2
    spot = {"x": lon % RING, "y": lon // RING, "z": lat // 2}
    names = ("first", "second", "third", "on", "core")
    sems = {name: (ring_sems[2 * n], ring_sems[2 * n + 1]) for n, name in enumerate(names)}
    gather = Gather(every_ref, sems, core, spot, lat, lon)

    loads = [
        pltpu.make_async_copy(src, dst, load_sem.at[n])
        for n, (src, dst) in enumerate(
            (
                (tok_hbm, tok_ref), (wq_hbm, wq_ref), (wk_hbm, wk_ref), (wv_hbm, wv_ref),
                (wout_hbm, wout_ref), (wup_hbm, wup_ref), (wdown_hbm, wdown_ref),
            )
        )
    ]
    for load in loads:
        load.start()

    def tile(lat_step, lon_step):
        return ((lat + lat_step + lats) % lats, (lon + lon_step + lons) % lons)

    halos = (
        (tok_hbm.at[BLK : 2 * BLK], up_ref, tile(1, 0)),
        (tok_hbm.at[0:BLK], down_ref, tile(-1, 0)),
        (tok_hbm.at[:, COLS - 1], left_ref, tile(0, 1)),
        (tok_hbm.at[:, 0], right_ref, tile(0, -1)),
        (tok_hbm.at[BLK : 2 * BLK, COLS - 1], corner_ref.at[0], tile(1, 1)),
        (tok_hbm.at[BLK : 2 * BLK, 0], corner_ref.at[1], tile(1, -1)),
        (tok_hbm.at[0:BLK, COLS - 1], corner_ref.at[2], tile(-1, 1)),
        (tok_hbm.at[0:BLK, 0], corner_ref.at[3], tile(-1, -1)),
    )
    halo_copies = [
        pltpu.make_async_remote_copy(
            src_ref=src, dst_ref=dst, send_sem=halo_send.at[n], recv_sem=halo_recv.at[n],
            device_id=device, device_id_type=MESH,
        )
        for n, (src, dst, device) in enumerate(halos)
    ]
    partners = [device for _, _, device in halos]
    partners += [gather.device(axis, step) for axis in ("x", "y", "z") for step in (1, -1, 2)]
    partners += [(lat + 1 - 2 * core, lon)]
    barrier = pltpu.get_barrier_semaphore()
    for partner in partners:
        pl.semaphore_signal(barrier, inc=1, device_id=partner, device_id_type=MESH)

    gain = gain_ref[...]
    pool_weight = pool_ref[...]

    ids = ids_ref[...]
    grow, gcol = ids >> 7, ids & 127
    to_lat, to_lon = grow >> 1, gcol >> 3
    to_spot = {"x": to_lon & 3, "y": to_lon >> 2, "z": to_lat >> 1}
    rows_ref[...] = jnp.zeros_like(rows_ref)
    rows_ref[:, :FAR] = summary_row(to_lat & 1, to_spot, (grow & 1) * COLS + (gcol & 7))
    index_load = pltpu.make_async_copy(rows_ref, idx_ref, load_sem.at[7])
    index_load.start()
    slot = lax.broadcasted_iota(jnp.int32, (FAR, FAR * SUMROWS), 0)
    key = lax.broadcasted_iota(jnp.int32, (FAR, FAR * SUMROWS), 1)
    spread = jnp.where(key // SUMROWS == slot, 1.0, 0.0).astype(BF16)
    used = jnp.where(mask_ref[...] > 0, 1.0, 0.0).astype(BF16)
    bias_ref[...] = jnp.where(dot(used, spread) > 0.5, 0.0, NEG)

    loads[0].wait()

    def block_of(ref, first, column):
        return jnp.concatenate([ref[first + r, column].astype(F32) for r in range(BLK)], axis=0)

    for part in range(3):
        base = gather.rows(part, 0, {}).start

        def pool_block(n, carry):
            b = n + FIRST[part]
            i, j = b // COLS, b % COLS
            normed = rms(block_of(tok_ref, i * BLK, j), gain)
            nb_ref[i + 1, pl.ds(pl.multiple_of((j + 1) * TOK, TOK), TOK), :] = normed
            every_ref[base + n] = dot(pool_weight, normed).astype(BF16)
            return carry

        lax.fori_loop(0, PARTS[part], pool_block, 0, unroll=True)
    pl.semaphore_wait(barrier, len(partners))
    gather.start_first()
    for copy in halo_copies:
        copy.start()

    inner = slice(TOK, TOK + ROW)
    loads[1].wait()
    loads[2].wait()
    loads[3].wait()

    def local_qkv(i):
        normed = nb_ref[i + 1, inner, :]
        q_ref[i] = dot(normed, wq_ref[...]).astype(BF16)
        k_ref[i + 1, inner, :] = dot(normed, wk_ref[...]).astype(BF16)
        v_ref[i + 1, inner, :] = dot(normed, wv_ref[...]).astype(BF16)

    local_qkv(0)
    gather.wait_first()
    gather.start_second()
    gather.start_third((0,))
    local_qkv(1)

    for copy in halo_copies:
        copy.wait_recv()

    def outer_kv(bi, rows):
        normed = nb_ref[bi, rows, :]
        k_ref[bi, rows, :] = dot(normed, wk_ref[...]).astype(BF16)
        v_ref[bi, rows, :] = dot(normed, wv_ref[...]).astype(BF16)

    last = slice(TOK + ROW, WIDE)
    first = slice(0, TOK)

    def outer_row(bi, ref, corner):
        def put(j, carry):
            rows = pl.ds(pl.multiple_of((j + 1) * TOK, TOK), TOK)
            nb_ref[bi, rows, :] = rms(block_of(ref, 0, j), gain)
            return carry

        lax.fori_loop(0, COLS, put, 0, unroll=2)
        for rows, n in ((first, corner), (last, corner + 1)):
            block = jnp.concatenate([corner_ref[n, r].astype(F32) for r in range(BLK)], axis=0)
            nb_ref[bi, rows, :] = rms(block, gain)
        outer_kv(bi, slice(0, WIDE))

    outer_row(0, up_ref, 0)
    gather.wait_second()
    gather.start_second_on()
    gather.start_third((1, 2))
    outer_row(3, down_ref, 2)
    for i in range(2):
        for ref, rows in ((left_ref, first), (right_ref, last)):
            block = jnp.concatenate([ref[i * BLK + r].astype(F32) for r in range(BLK)], axis=0)
            nb_ref[i + 1, rows, :] = rms(block, gain)
            outer_kv(i + 1, rows)

    lane_head = lax.broadcasted_iota(jnp.int32, (TOK, 256), 1) // TOK

    def stacked_query(i, rows, feats):
        query = q_ref[i, rows, feats]
        zero = jnp.zeros_like(query)
        return jnp.concatenate([jnp.where(lane_head == h, query, zero) for h in range(4)], axis=0)

    def scores(query, keys):
        return lax.dot_general(query, keys, (((1,), (1,)), ((), ())), preferred_element_type=F32)

    def soft_sum(score, values, scales, bias):
        weights, highs, totals = [], [], []
        for h in range(4):
            part = bias(score[h * TOK : (h + 1) * TOK])
            highest = jnp.max(part, axis=-1, keepdims=True)
            expo = jnp.exp2((part - highest) * scales[h])
            highs.append(highest)
            totals.append(jnp.sum(expo, axis=-1, keepdims=True))
            weights.append(expo.astype(BF16))
        full = dot(jnp.concatenate(weights, axis=0), values)
        picked = full[0:TOK]
        high = jnp.broadcast_to(highs[0], (TOK, 256))
        total = jnp.broadcast_to(totals[0], (TOK, 256))
        for h in range(1, 4):
            mine = lane_head == h
            picked = jnp.where(mine, full[h * TOK : (h + 1) * TOK], picked)
            high = jnp.where(mine, highs[h], high)
            total = jnp.where(mine, totals[h], total)
        return picked, high, total

    def near_block(b, carry):
        i, j = b // COLS, b % COLS
        start = pl.multiple_of(j * TOK, TOK)
        rows = pl.ds(start, TOK)
        around = pl.ds(start, 3 * TOK)
        inside = jnp.where(i == 0, lat > 0, lat < lats - 1)
        edge = jnp.where(inside, jnp.float32(0.0), jnp.float32(NEG))
        for g in range(2):
            feats = slice(g * 256, (g + 1) * 256)
            keys = jnp.concatenate([k_ref[d, around, feats] for d in (1, 2, 3 * i)], axis=0)
            values = jnp.concatenate([v_ref[d, around, feats] for d in (1, 2, 3 * i)], axis=0)
            score = scores(stacked_query(i, rows, feats), keys)
            near_ref[i, rows, feats], high_ref[i, rows, feats], total_ref[i, rows, feats] = soft_sum(
                score, values, [head_ref[0, g * 4 + h] * SCALE for h in range(4)],
                lambda part: jnp.concatenate([part[:, :384], part[:, 384:] + edge], axis=1),
            )
        return carry

    def pump_s():
        gather.wait_second_on()
        gather.start_third((3,))
        gather.start_sibling((0,))
        gather.wait_third((0,))
        gather.start_third_on((0,))

    def pump_a():
        gather.wait_third((1, 2))
        gather.start_third_on((1, 2))

    def pump_b():
        gather.wait_third((3,))
        gather.start_third_on((3,))
        gather.start_sibling((1, 2))

    def pump_c():
        gather.wait_third_on((0, 1))
        gather.start_sibling((3, 4))

    def pump_d():
        gather.wait_third_on((2, 3))
        gather.start_sibling((5, 6))

    pumps = ((PUMP_S, pump_s), (PUMP_A, pump_a), (PUMP_B, pump_b), (PUMP_C, pump_c), (PUMP_D, pump_d))

    def near_step(b, carry):
        for when, pump in pumps:
            pl.when(b == when)(pump)
        return near_block(b, carry)

    lax.fori_loop(0, 16, near_step, 0)
    gather.wait_sibling(range(7))
    index_load.wait()

    def far_block(b, carry):
        i, j = b // COLS, b % COLS
        rows = pl.ds(pl.multiple_of(j * TOK, TOK), TOK)
        for s in range(FAR):
            far_ref[s * SUMROWS : (s + 1) * SUMROWS, :] = every_ref[idx_ref[b, s]]
        far = far_ref[...]
        keys = dot(far, wk_ref[...]).astype(BF16)
        values = dot(far, wv_ref[...]).astype(BF16)
        bias = bias_ref[pl.ds(b, 1), :]
        for g in range(2):
            feats = slice(g * 256, (g + 1) * 256)
            score = scores(stacked_query(i, rows, feats), keys[:, feats])
            scales = [head_ref[0, g * 4 + h] * SCALE for h in range(4)]
            far_sum, far_high, far_total = soft_sum(
                score, values[:, feats], scales, lambda part: part + bias
            )
            scale = jnp.full((1, 256), scales[0], F32)
            for h in range(1, 4):
                scale = jnp.where(lane_head[:1] == h, scales[h], scale)
            near_high = high_ref[i, rows, feats]
            high = jnp.maximum(near_high, far_high)
            near_part = jnp.exp2((near_high - high) * scale)
            far_part = jnp.exp2((far_high - high) * scale)
            total = total_ref[i, rows, feats] * near_part + far_total * far_part
            mixed = near_ref[i, rows, feats] * near_part + far_sum * far_part
            attn_ref[i, rows, feats] = (mixed / total).astype(BF16)
        return carry

    lax.fori_loop(0, 16, far_block, 0, unroll=2)

    for load in loads[4:]:
        load.wait()
    mgain = mgain_ref[...]

    def feed_forward(t, carry):
        i, half = t // 2, t % 2
        rows = pl.ds(pl.multiple_of(half * 256, 256), 256)
        token = jnp.concatenate(
            [block_of(tok_ref, i * BLK, half * 4 + j) for j in range(4)], axis=0
        )
        mixed = (token + dot(attn_ref[i, rows, :], wout_ref[...])).astype(BF16)
        wide = mixed.astype(F32)
        normed = rms(wide, mgain)
        acc = wide
        for f in range(4):
            part = slice(f * 512, (f + 1) * 512)
            hidden = jax.nn.gelu(dot(normed, wup_ref[:, part]), approximate=True).astype(BF16)
            acc = acc + dot(hidden, wdown_ref[part, :])
        for r in range(BLK):
            row = jnp.concatenate(
                [acc[j * TOK + r * BLK : j * TOK + (r + 1) * BLK] for j in range(4)], axis=0
            )
            out_ref[i * BLK + r, pl.ds(pl.multiple_of(half * 32, 32), 32), :] = row.astype(BF16)
        return carry

    lax.fori_loop(0, 4, feed_forward, 0, unroll=2)
    for copy in halo_copies:
        copy.wait_send()
    gather.finish()


def layer_call(head_scale, ids, mask, gain, mgain, pool_weight, tokens, weights):
    rows, cols, feature = tokens.shape
    vmem = pl.BlockSpec(memory_space=pltpu.VMEM)
    smem = pl.BlockSpec(memory_space=pltpu.SMEM)
    hbm = pl.BlockSpec(memory_space=pl.ANY)
    half = (BLK, COLS, BLK, feature)
    dma = pltpu.SemaphoreType.DMA
    return pl.pallas_call(
        layer_kernel,
        out_shape=jax.ShapeDtypeStruct(tokens.shape, BF16),
        in_specs=[smem] + [vmem] * 5 + [hbm] * 7,
        out_specs=vmem,
        scratch_shapes=[
            pltpu.VMEM((2 * BLK, COLS, BLK, feature), BF16),
            pltpu.VMEM(half, BF16),
            pltpu.VMEM(half, BF16),
            pltpu.VMEM((2 * BLK, BLK, feature), BF16),
            pltpu.VMEM((2 * BLK, BLK, feature), BF16),
            pltpu.VMEM((4, BLK, BLK, feature), BF16),
        ]
        + [pltpu.VMEM(weight.shape, BF16) for weight in weights]
        + [
            pltpu.VMEM((2048, SUMROWS, feature), BF16),
            pltpu.VMEM((4, WIDE, feature), BF16),
            pltpu.VMEM((2, ROW, feature), BF16),
            pltpu.VMEM((4, WIDE, feature), BF16),
            pltpu.VMEM((4, WIDE, feature), BF16),
            pltpu.VMEM((FAR * SUMROWS, feature), BF16),
            pltpu.VMEM((2, ROW, feature), F32),
            pltpu.VMEM((2, ROW, feature), F32),
            pltpu.VMEM((2, ROW, feature), F32),
            pltpu.VMEM((2, ROW, feature), BF16),
            pltpu.VMEM((2 * COLS, 128), jnp.int32),
            pltpu.SMEM((2 * COLS, 128), jnp.int32),
            pltpu.VMEM((2 * COLS, FAR * SUMROWS), F32),
            dma((8,)), dma((8,)), dma((8,)),
        ]
        + [dma(shape) for shape in ((3, 3), (3, 4), (3, 4, 2), (3, 4), (3, 7)) for _ in range(2)],
        compiler_params=pltpu.CompilerParams(
            vmem_limit_bytes=60 << 20, collective_id=0, has_side_effects=True
        ),
        name="layer",
    )(
        head_scale, ids, mask, gain.reshape(1, feature), mgain.reshape(1, feature), pool_weight,
        tokens.reshape(rows, COLS, BLK, feature), *weights,
    )


def local(
    tokens, norm_gain, w_query, w_key, w_value, w_out, pool_weight, head_scale,
    far_ids, far_mask, mlp_gain, w_up, w_down,
):
    return layer_call(
        head_scale.reshape(1, -1), far_ids.reshape(-1, FAR), far_mask.reshape(-1, FAR),
        norm_gain, mlp_gain, pool_weight, tokens,
        (w_query, w_key, w_value, w_out, w_up, w_down),
    )


def solution(mesh):
    return jax.shard_map(
        local,
        mesh=mesh,
        in_specs=(
            P("lat", "lon", None),
            P(), P(), P(), P(), P(), P(), P(),
            P("lat", "lon", None),
            P("lat", "lon", None),
            P(), P(), P(),
        ),
        out_specs=P("lat", "lon", None),
        check_vma=False,
    )
```
